256 devices in a mesh: dp: 16 (over z_hi, y), freq: 16 (over z_lo, x, core).
Axes of the slice: x: 4, y: 4, z: 8 (z_hi: 4, z_lo: 2; z = z_hi * 2 + z_lo), core: 2. Of those that a mesh axis runs over, the one named last changes fastest.
Arguments:
- noisy: bfloat16 [16, 4096, 2, 512], P('dp', 'freq'), may hold values from -6 to 6
- timestep: int32 [16], P('dp'), may hold values from 0 to 999
- kernel: float32 [3, 3, 512], replicated, may hold values from -2 to 2
- film_weight: bfloat16 [512, 1024], replicated, may hold values from -0.25 to 0.25
- mixing: bfloat16 [4096, 4096], P('freq'), may hold values from -0.09375 to 0.09375
- cotangent: bfloat16 [16, 4096, 2, 512], P('dp', 'freq'), may hold values from -6 to 6
Outputs:
- output: bfloat16 [16, 4096, 2, 512], P('dp', 'freq')
- grad_noisy: bfloat16 [16, 4096, 2, 512], P('dp', 'freq')
- grad_mixing: float32 [4096, 4096], P('freq')
- grad_kernel: float32 [3, 3, 512], replicated
- grad_film: float32 [512, 1024], replicated
The draws below stay inside these ranges and needn't reach their ends.
All inputs are finite; a program needn't handle non-finite values.
Results may differ from the reference program's by a relative error of at most 0.005.
Values may be sent and summed in bfloat16 or wider, within the bound.
A program may use at most 128 MiB of HBM per device.

```python
import math
import jax
import jax.numpy as jnp
from jax import lax

F = 4096
C = 512
FRAMES = 2
STEPS = 1000
RECORDS = 16


def place_ends(array, rng, smallest, top_value):
    spot = [jax.random.randint(jax.random.fold_in(rng, axis), (), 0, length) for axis, length in enumerate(array.shape)]
    main_axis = array.shape.index(max(array.shape))
    neighbour = spot[:main_axis] + [(spot[main_axis] + 1) % array.shape[main_axis]] + spot[main_axis + 1:]
    return array.at[tuple(spot)].set(smallest).at[tuple(neighbour)].set(top_value)


def level_of(key, dims, shards, least, top_value):
    factor_of, own = 1.0, jax.random.fold_in(key, 6)
    for position, blocks in shards:
        draws = jnp.exp(jax.random.uniform(jax.random.fold_in(own, position), (blocks,), jnp.float32, least / len(shards), top_value / len(shards)))
        factor_of = factor_of * jnp.repeat(draws, dims[position] // blocks).reshape([-1 if axis == position else 1 for axis in range(len(dims))])
    return factor_of


def gaussian(rng, extent, deviation, limit, split=(), kind=jnp.bfloat16):
    entries = jax.random.normal(rng, extent, jnp.float32) * deviation
    if len(split) > 0:
        entries = level_of(rng, extent, split, -0.22, 0.18) * entries
    return jnp.clip(entries, min=-limit, max=limit).astype(kind)


def setup_inputs(seed: int = 0) -> dict:
    splits = jax.random.split(jax.random.key(seed), 7)
    noisy = gaussian(splits[0], (RECORDS, F, FRAMES, C), 1.0, 6.0, ((0, 16), (1, 16)))
    timestep = place_ends(jax.random.randint(splits[1], (RECORDS,), 0, STEPS), jax.random.fold_in(splits[1], 1), 0, STEPS - 1).astype(jnp.int32)
    kernel = gaussian(splits[2], (3, 3, C), 9 ** -0.5, 2.0, (), jnp.float32)
    film_weight = gaussian(splits[3], (C, 2 * C), C ** -0.5, 0.25)
    mixing = gaussian(splits[4], (F, F), F ** -0.5, 0.09375, ((0, 16),))
    cotangent = gaussian(splits[5], (RECORDS, F, FRAMES, C), 1.0, 6.0, ((0, 16), (1, 16)))
    return dict(noisy=noisy, timestep=timestep, kernel=kernel, film_weight=film_weight, mixing=mixing, cotangent=cotangent)


def embed_steps(timestep):
    half = C // 2
    freqs = jnp.exp(-math.log(10000.0) * jnp.arange(half, dtype=jnp.float32) / half)
    angles = timestep.astype(jnp.float32)[:, None] * freqs[None, :]
    return jnp.concatenate([jnp.sin(angles), jnp.cos(angles)], axis=1).astype(jnp.bfloat16)

def reference(noisy, timestep, kernel, film_weight, mixing, cotangent):
    embed = embed_steps(timestep)
    film = jnp.dot(embed, film_weight, preferred_element_type=jnp.float32)
    scale = film[:, :C][:, None, None, :]
    shift = film[:, C:][:, None, None, :]
    noisy_wide = noisy.astype(jnp.float32)
    padded = jnp.pad(noisy_wide, ((0, 0), (1, 1), (1, 1), (0, 0)))
    stencil = jnp.zeros_like(noisy_wide)
    for row_off in range(3):
        for col_off in range(3):
            stencil = stencil + kernel[row_off, col_off] * padded[:, row_off:row_off + F, col_off:col_off + FRAMES]
    rinv = lax.rsqrt(lax.optimization_barrier(jnp.mean(stencil * stencil, axis=-1, keepdims=True)) + 1e-05)
    normed = stencil * rinv
    act = normed * (1.0 + scale) + shift
    gated = jax.nn.silu(act).astype(jnp.bfloat16)
    mixing_wide = mixing.astype(jnp.float32)
    mixed = jnp.einsum('pf,bftc->bptc', mixing_wide, gated.astype(jnp.float32))
    output = (noisy_wide + mixed).astype(jnp.bfloat16)
    grad_gated = jnp.einsum('pf,bptc->bftc', mixing_wide, cotangent.astype(jnp.float32))
    grad_mixing = jnp.einsum('bptc,bftc->pf', cotangent.astype(jnp.float32), gated.astype(jnp.float32))
    sig = jax.nn.sigmoid(act)
    grad_act = grad_gated * sig * (1.0 + act * (1.0 - sig))
    grad_scale = lax.optimization_barrier(jnp.sum(grad_act * normed, axis=(1, 2)))
    grad_shift = lax.optimization_barrier(jnp.sum(grad_act, axis=(1, 2)))
    grad_normed = grad_act * (1.0 + scale)
    grad_stencil = rinv * (grad_normed - normed * lax.optimization_barrier(jnp.mean(grad_normed * normed, axis=-1, keepdims=True)))
    grad_padded = jnp.pad(grad_stencil, ((0, 0), (1, 1), (1, 1), (0, 0)))
    back = jnp.zeros_like(noisy_wide)
    grad_kernel_rows = []
    for row_off in range(3):
        kernel_cols = []
        for col_off in range(3):
            back = back + kernel[row_off, col_off] * grad_padded[:, 2 - row_off:2 - row_off + F, 2 - col_off:2 - col_off + FRAMES]
            kernel_cols.append(lax.optimization_barrier(jnp.sum(padded[:, row_off:row_off + F, col_off:col_off + FRAMES] * grad_stencil, axis=(0, 1, 2))))
        grad_kernel_rows.append(jnp.stack(kernel_cols))
    grad_kernel = jnp.stack(grad_kernel_rows)
    grad_noisy = (cotangent.astype(jnp.float32) + back).astype(jnp.bfloat16)
    grad_both = jnp.concatenate([grad_scale, grad_shift], axis=1)
    grad_film = jnp.dot(embed.astype(jnp.float32).T, grad_both, precision=lax.Precision.HIGHEST)
    return (output, grad_noisy, grad_mixing, grad_kernel, grad_film)
```

```python
import functools
import math

import jax
import jax.numpy as jnp
from jax import lax
from jax.experimental import pallas as pl
from jax.experimental.pallas import tpu as pltpu
from jax.sharding import PartitionSpec as P

MESH = pl.DeviceIdType.MESH
BAND = 256
C = 512
NT = 2
ROWS = 16
F32 = jnp.float32
BF16 = jnp.bfloat16


class Places:
    def __init__(self):
        self.dp = lax.axis_index("dp")
        self.fr = lax.axis_index("freq")
        self.zh, self.y = self.dp // 4, self.dp % 4
        self.zl, self.x, self.c = self.fr // 8, (self.fr // 2) % 4, self.fr % 2

    def qpos(self, k):
        zl = self.zl if k < 2 else 1 - self.zl
        c = self.c if k % 2 == 0 else 1 - self.c
        return zl, c

    def q(self, k):
        zl, c = self.qpos(k)
        return (self.dp, zl * 8 + self.x * 2 + c)

    def xp(self, k):
        return (self.dp, self.zl * 8 + ((self.x + k) % 4) * 2 + self.c)

    def yp(self, k):
        return (self.zh * 4 + (self.y + k) % 4, self.fr)

    def zp(self, k):
        return (((self.zh + k) % 4) * 4 + self.y, self.fr)

    def nb(self, k):
        return (self.dp, (self.fr + 16 + k) % 16)


def sigmoid(a):
    return 1.0 / (1.0 + jnp.exp(-a))


def block_kernel(
    noisy, cot, mixing, film, embed, kern,
    out_o, gn_o, gm_o, gat_o,
    npad, nlo, nhi, normed, rinv, ga, ca, mx,
    psend, precv, pown, osend, orecv, oown,
    gms, yr, ys, zr, zs, fx,
    gs, gkacc, sm, smq, smx, smr, smt,
    ssem, rsem, lsem,
):
    me = Places()
    barrier = pltpu.get_barrier_semaphore()
    peers = [f(k) for f in (me.q, me.xp, me.yp, me.zp) for k in (1, 2, 3)]
    peers += [me.nb(1), me.nb(-1)]
    for peer in peers:
        pl.semaphore_signal(barrier, inc=1, device_id=peer, device_id_type=MESH)
    pl.semaphore_wait(barrier, len(peers))

    copies = []

    def rcopy(src, dst, dev):
        i = len(copies)
        copy = pltpu.make_async_remote_copy(
            src_ref=src, dst_ref=dst, send_sem=ssem.at[i], recv_sem=rsem.at[i],
            device_id=dev, device_id_type=MESH,
        )
        copies.append(copy)
        copy.start()
        return copy

    halo_in = [
        rcopy(noisy.at[:, pl.ds(0, 16), :], nhi, me.nb(-1)),
        rcopy(noisy.at[:, pl.ds(BAND - 16, 16), :], nlo, me.nb(1)),
    ]
    cot_in = [rcopy(cot, ca.at[:, pl.ds(k * BAND, BAND), :], me.q(k)) for k in (1, 2, 3)]

    def mix_cols(k, j):
        zl, c = me.qpos(k)
        band = zl * 8 + ((me.x + j) % 4) * 2 + c
        return mixing.at[:, pl.ds(pl.multiple_of(band * BAND, BAND), BAND)]

    def mix_slot(k, j):
        return mx.at[pl.ds(k * BAND, BAND), pl.ds(j * BAND, BAND)]

    mix_in = [
        rcopy(mix_cols(k, j), mix_slot(k, j), me.q(k)) for k in (1, 2, 3) for j in range(4)
    ]
    local = []
    for j in range(4):
        local.append(pltpu.make_async_copy(mix_cols(0, j), mix_slot(0, j), lsem.at[j]))
    local.append(pltpu.make_async_copy(cot, ca.at[:, pl.ds(0, BAND), :], lsem.at[4]))
    for copy in local:
        copy.start()

    for copy in halo_in:
        copy.wait_recv()
    low_on = jnp.where(me.fr > 0, 1.0, 0.0).astype(F32)
    high_on = jnp.where(me.fr < 15, 1.0, 0.0).astype(F32)
    for t in range(NT):
        npad[t, 0:8, :] = nlo[t].astype(F32)[8:16] * low_on
        npad[t, BAND + 8 : BAND + 16, :] = nhi[t].astype(F32)[0:8] * high_on

    @pl.loop(0, BAND // ROWS)
    def _(r):
        base = pl.multiple_of(r * ROWS, ROWS)
        for t in range(NT):
            npad[t, pl.ds(base + 8, ROWS), :] = noisy[t, pl.ds(base, ROWS), :].astype(F32)

    scale1 = film[0:1, :]
    shift = film[1:2, :]

    def forward_rows(r):
        base = pl.multiple_of(r * ROWS, ROWS)
        wins = []
        for t in range(NT):
            w = npad[t, pl.ds(base, ROWS + 16), :]
            wins.append([w[7 + i : 7 + i + ROWS] for i in range(3)])
        for t in range(NT):
            st = None
            for tp in range(NT):
                for i in range(3):
                    term = kern[i * 3 + tp - t + 1][None, :] * wins[tp][i]
                    st = term if st is None else st + term
            ri = lax.rsqrt(jnp.mean(st * st, axis=-1, keepdims=True) + 1e-05)
            nm = st * ri
            normed[t, pl.ds(base, ROWS), :] = nm
            rinv[t, pl.ds(base, ROWS), :] = jnp.broadcast_to(ri, (ROWS, 128))
            act = nm * scale1 + shift
            ga[t, pl.ds(base, ROWS), :] = (act * sigmoid(act)).astype(BF16)

    half = BAND // 2
    gate_in = []
    for h in range(2):
        pl.loop(h * half // ROWS, (h + 1) * half // ROWS)(forward_rows)
        for k in (1, 3, 2):
            gate_in.append(
                (
                    4 - k,
                    rcopy(
                        ga.at[:, pl.ds(h * half, half), :],
                        ga.at[:, pl.ds((4 - k) * BAND + h * half, half), :],
                        me.xp(k),
                    ),
                )
            )

    def mixing_grad(j):
        @pl.loop(0, 4)
        def _(k):
            rows = pl.ds(pl.multiple_of(k * BAND, BAND), BAND)
            acc = None
            for t in range(NT):
                part = lax.dot_general(
                    ca[t, rows, :], ga[t, pl.ds(j * BAND, BAND), :],
                    (((1,), (1,)), ((), ())), preferred_element_type=F32,
                )
                acc = part if acc is None else acc + part
            gms[j, k] = acc.astype(BF16)

        sent = []
        for m in (1, 2, 3):
            y2 = (me.y + m) % 4
            rows = pl.ds(pl.multiple_of(y2 * 64, 64), 64)
            sent.append(rcopy(gms.at[j, :, rows, :], yr.at[j, m - 1], me.yp(m)))
        return sent

    for copy in cot_in:
        copy.wait_recv()
    for copy in local:
        copy.wait()
    y_in = {0: mixing_grad(0)}

    for copy in mix_in:
        copy.wait_recv()

    def gate_grad(j):
        mt = mx[:, pl.ds(j * BAND, BAND)].T
        return [jnp.dot(mt, ca[t], preferred_element_type=F32) for t in range(NT)]

    p_in = []
    for j in (1, 3, 2):
        parts = gate_grad(j)
        for t in range(NT):
            psend[j - 1, t] = parts[t].astype(BF16)
        p_in.append(rcopy(psend.at[j - 1], precv.at[j - 1], me.xp(j)))
    parts = gate_grad(0)
    for t in range(NT):
        pown[t] = parts[t]

    for j in (3, 1, 2):
        for slot, copy in gate_in:
            if slot == j:
                copy.wait_recv()
        y_in[j] = mixing_grad(j)

    def mixed(k, t):
        return jnp.dot(mx[pl.ds(k * BAND, BAND), :], ga[t], preferred_element_type=F32)

    o_in = []
    for k in (2, 3, 1):
        for t in range(NT):
            osend[k - 1, t] = mixed(k, t).astype(BF16)
        o_in.append(rcopy(osend.at[k - 1], orecv.at[k - 1], me.q(k)))
    for t in range(NT):
        oown[t] = mixed(0, t)

    def y_sum(j):
        for copy in y_in[j]:
            copy.wait_recv()
        rows = pl.ds(pl.multiple_of(me.y * 64, 64), 64)
        for k in range(4):
            total = gms[j, k, rows, :].astype(F32)
            for m in range(3):
                total = total + yr[j, m, k].astype(F32)
            ys[j, k] = total.astype(BF16)
        sent = []
        for m in (1, 2, 3):
            z2 = (me.zh + m) % 4
            rows = pl.ds(pl.multiple_of(z2 * 16, 16), 16)
            sent.append(rcopy(ys.at[j, :, rows, :], zr.at[j, m - 1], me.zp(m)))
        return sent

    z_in = {}
    for j in (0, 3, 1):
        z_in[j] = y_sum(j)

    for copy in p_in:
        copy.wait_recv()
    gkacc[...] = jnp.zeros_like(gkacc)

    @pl.loop(0, BAND // ROWS)
    def _(r):
        base = pl.multiple_of(r * ROWS, ROWS)
        rows = pl.ds(base, ROWS)
        for t in range(NT):
            gg = pown[t, rows, :]
            for m in range(3):
                gg = gg + precv[m, t, rows, :].astype(F32)
            nm = normed[t, rows, :]
            ri = rinv[t, rows, :][:, 0:1]
            act = nm * scale1 + shift
            sig = sigmoid(act)
            gact = gg * sig * (1.0 + act * (1.0 - sig))
            prod = gact * nm
            gkacc[9] += prod[0:8] + prod[8:16]
            gkacc[10] += gact[0:8] + gact[8:16]
            gnm = gact * scale1
            mean = jnp.mean(gnm * nm, axis=-1, keepdims=True)
            gs[t, pl.ds(base + 8, ROWS), :] = ri * (gnm - nm * mean)

    halo_gs = [
        rcopy(gs.at[:, pl.ds(8, 8), :], gs.at[:, pl.ds(BAND + 8, 8), :], me.nb(-1)),
        rcopy(gs.at[:, pl.ds(BAND, 8), :], gs.at[:, pl.ds(0, 8), :], me.nb(1)),
    ]

    z_in[2] = y_sum(2)

    rows16 = pl.ds(pl.multiple_of(me.zh * 16, 16), 16)
    for j in (0, 3, 1, 2):
        for copy in z_in[j]:
            copy.wait_recv()
        for k in range(4):
            total = ys[j, k, rows16, :].astype(F32)
            for m in range(3):
                total = total + zr[j, m, k].astype(F32)
            zs[k, j] = total.astype(BF16)
    f_in = [rcopy(zs.at[k], fx.at[k - 1], me.q(k)) for k in (1, 2, 3)]

    for copy in o_in:
        copy.wait_recv()

    @pl.loop(0, BAND // ROWS)
    def _(r):
        rows = pl.ds(pl.multiple_of(r * ROWS, ROWS), ROWS)
        for t in range(NT):
            total = oown[t, rows, :] + noisy[t, rows, :].astype(F32)
            for m in range(3):
                total = total + orecv[m, t, rows, :].astype(F32)
            out_o[t, rows, :] = total.astype(BF16)

    mine = pl.ds(pl.multiple_of(me.y * 64 + me.zh * 16, 16), 16)
    for copy in f_in:
        copy.wait_recv()
    for k in range(4):
        zl, c = me.qpos(k)
        for j in range(4):
            band = zl * 8 + ((me.x + j) % 4) * 2 + c
            cols = pl.ds(pl.multiple_of(band * BAND, BAND), BAND)
            gm_o[mine, cols] = zs[0, j] if k == 0 else fx[k - 1, j]
    az_in = [rcopy(gm_o.at[mine, :], gm_o.at[mine, :], me.zp(m)) for m in (1, 2, 3)]

    for copy in halo_gs:
        copy.wait()
    for t in range(NT):
        gs[t, 0:8, :] = gs[t, 0:8, :] * low_on
        gs[t, BAND + 8 : BAND + 16, :] = gs[t, BAND + 8 : BAND + 16, :] * high_on

    @pl.loop(0, BAND // ROWS)
    def _(r):
        base = pl.multiple_of(r * ROWS, ROWS)
        rows = pl.ds(base, ROWS)
        wins = []
        for t in range(NT):
            w = gs[t, pl.ds(base, ROWS + 16), :]
            wins.append([w[9 - i : 9 - i + ROWS] for i in range(3)])
        for tp in range(NT):
            ns = noisy[tp, rows, :].astype(F32)
            back = cot[tp, rows, :].astype(F32)
            for t in range(NT):
                for i in range(3):
                    spot = i * 3 + tp - t + 1
                    w = wins[t][i]
                    back = back + kern[spot][None, :] * w
                    prod = ns * w
                    gkacc[spot] += prod[0:8] + prod[8:16]
            gn_o[tp, rows, :] = back.astype(BF16)

    sm[...] = jnp.zeros_like(sm)
    for i in range(11):
        sm[i : i + 1, :] = jnp.sum(gkacc[i], axis=0, keepdims=True)
    smq_in = [rcopy(sm, smq.at[k - 1], me.q(k)) for k in (1, 2, 3)]

    for copy in az_in:
        copy.wait_recv()
    yrows = pl.ds(pl.multiple_of(me.y * 64, 64), 64)
    ay_in = [rcopy(gm_o.at[yrows, :], gm_o.at[yrows, :], me.yp(m)) for m in (1, 2, 3)]

    for copy in smq_in:
        copy.wait_recv()
    smt[...] = sm[...] + smq[0] + smq[1] + smq[2]
    smx_in = [rcopy(smt, smx.at[k - 1], me.xp(k)) for k in (1, 2, 3)]
    for copy in smx_in:
        copy.wait_recv()
    smr[...] = smt[...] + smx[0] + smx[1] + smx[2]
    smr[11:12, :] = embed[0:1, :]
    gat_o[me.dp] = smr[...]
    gy_in = [rcopy(smr, gat_o.at[me.dp], me.yp(m)) for m in (1, 2, 3)]
    for copy in gy_in:
        copy.wait_recv()
    four = pl.ds(me.zh * 4, 4)
    gz_in = [rcopy(gat_o.at[four], gat_o.at[four], me.zp(m)) for m in (1, 2, 3)]
    for copy in gz_in:
        copy.wait_recv()
    for copy in ay_in:
        copy.wait_recv()
    waited = set(id(copy) for copy in halo_gs)
    for copy in copies:
        if id(copy) not in waited:
            copy.wait_send()


N_COPIES = 2 + 3 + 12 + 6 + 12 + 3 + 3 + 12 + 2 + 3 + 3 + 3 + 3 + 3 + 3 + 3


def fused_block(noisy, cot, mixing, film, embed, kern):
    vmem = pl.BlockSpec(memory_space=pltpu.VMEM)
    hbm = pl.BlockSpec(memory_space=pl.ANY)
    act = (NT, BAND, C)
    full = (NT, 4 * BAND, C)
    pad = (NT, BAND + 16, C)
    return pl.pallas_call(
        block_kernel,
        out_shape=(
            jax.ShapeDtypeStruct(act, BF16),
            jax.ShapeDtypeStruct(act, BF16),
            jax.ShapeDtypeStruct((BAND, 16 * BAND), BF16),
            jax.ShapeDtypeStruct((16, 16, C), F32),
        ),
        in_specs=[vmem, vmem, hbm, vmem, vmem, vmem],
        out_specs=(vmem, vmem, vmem, vmem),
        scratch_shapes=[
            pltpu.VMEM(pad, F32),
            pltpu.VMEM((NT, 16, C), BF16),
            pltpu.VMEM((NT, 16, C), BF16),
            pltpu.VMEM(act, F32),
            pltpu.VMEM((NT, BAND, 128), F32),
            pltpu.VMEM(full, BF16),
            pltpu.VMEM(full, BF16),
            pltpu.VMEM((4 * BAND, 4 * BAND), BF16),
            pltpu.VMEM((3,) + act, BF16),
            pltpu.VMEM((3,) + act, BF16),
            pltpu.VMEM(act, F32),
            pltpu.VMEM((3,) + act, BF16),
            pltpu.VMEM((3,) + act, BF16),
            pltpu.VMEM(act, F32),
            pltpu.VMEM((4, 4, BAND, BAND), BF16),
            pltpu.VMEM((4, 3, 4, 64, BAND), BF16),
            pltpu.VMEM((4, 4, 64, BAND), BF16),
            pltpu.VMEM((4, 3, 4, 16, BAND), BF16),
            pltpu.VMEM((4, 4, 16, BAND), BF16),
            pltpu.VMEM((3, 4, 16, BAND), BF16),
            pltpu.VMEM(pad, F32),
            pltpu.VMEM((11, 8, C), F32),
            pltpu.VMEM((16, C), F32),
            pltpu.VMEM((3, 16, C), F32),
            pltpu.VMEM((3, 16, C), F32),
            pltpu.VMEM((16, C), F32),
            pltpu.VMEM((16, C), F32),
            pltpu.SemaphoreType.DMA((N_COPIES,)),
            pltpu.SemaphoreType.DMA((N_COPIES,)),
            pltpu.SemaphoreType.DMA((5,)),
        ],
        compiler_params=pltpu.CompilerParams(
            collective_id=0, has_side_effects=True, vmem_limit_bytes=60 * 1024 * 1024
        ),
    )(noisy, cot, mixing, film, embed, kern)


def embed_steps(timestep, width):
    half = width // 2
    freqs = jnp.exp(-math.log(10000.0) * jnp.arange(half, dtype=jnp.float32) / half)
    angles = timestep.astype(jnp.float32)[:, None] * freqs[None, :]
    return jnp.concatenate([jnp.sin(angles), jnp.cos(angles)], axis=1).astype(jnp.bfloat16)


def on_device(noisy, timestep, kernel, film_weight, mixing, cotangent):
    embed = embed_steps(timestep, C)
    film = jnp.dot(embed, film_weight, preferred_element_type=jnp.float32)
    film = jnp.concatenate([1.0 + film[:, :C], film[:, C:]], axis=0)
    planes = [jnp.transpose(a[0], (1, 0, 2)) for a in (noisy, cotangent)]
    out, grad_noisy, grad_mixing, gathered = fused_block(
        planes[0], planes[1], mixing, film, embed.astype(F32), kernel.reshape(9, C)
    )
    output = jnp.transpose(out, (1, 0, 2))[None]
    grad_noisy = jnp.transpose(grad_noisy, (1, 0, 2))[None]
    grad_kernel = jnp.sum(gathered[:, :9], axis=0).reshape(3, 3, C)
    both = jnp.concatenate([gathered[:, 9], gathered[:, 10]], axis=1)
    grad_film = jnp.dot(gathered[:, 11].T, both, precision=lax.Precision.HIGHEST)
    return (output, grad_noisy, grad_mixing.astype(F32), grad_kernel, grad_film)


def solution(mesh):
    return jax.shard_map(
        on_device,
        mesh=mesh,
        in_specs=(
            P("dp", "freq", None, None),
            P("dp"),
            P(),
            P(),
            P("freq", None),
            P("dp", "freq", None, None),
        ),
        out_specs=(
            P("dp", "freq", None, None),
            P("dp", "freq", None, None),
            P("freq", None),
            P(),
            P(),
        ),
        check_vma=False,
    )
```

```python
import functools
import math

import jax
import jax.numpy as jnp
from jax import lax
from jax.experimental import pallas as pl
from jax.experimental.pallas import tpu as pltpu
from jax.sharding import PartitionSpec as P

MESH = pl.DeviceIdType.MESH
BAND = 256
C = 512
NT = 2
ROWS = 16
F32 = jnp.float32
BF16 = jnp.bfloat16


class Places:
    def __init__(self):
        self.dp = lax.axis_index("dp")
        self.fr = lax.axis_index("freq")
        self.zh, self.y = self.dp // 4, self.dp % 4
        self.zl, self.x, self.c = self.fr // 8, (self.fr // 2) % 4, self.fr % 2

    def qpos(self, k):
        zl = self.zl if k < 2 else 1 - self.zl
        c = self.c if k % 2 == 0 else 1 - self.c
        return zl, c

    def q(self, k):
        zl, c = self.qpos(k)
        return (self.dp, zl * 8 + self.x * 2 + c)

    def xp(self, k):
        return (self.dp, self.zl * 8 + ((self.x + k) % 4) * 2 + self.c)

    def yp(self, k):
        return (self.zh * 4 + (self.y + k) % 4, self.fr)

    def zp(self, k):
        return (((self.zh + k) % 4) * 4 + self.y, self.fr)

    def zo(self, k):
        zl, c = self.qpos(k)
        zh = (self.zh + jnp.where(self.zl == 1, 1, 3)) % 4
        return (zh * 4 + self.y, zl * 8 + self.x * 2 + c)

    def nb(self, k):
        return (self.dp, (self.fr + 16 + k) % 16)


def sigmoid(a):
    return 1.0 / (1.0 + jnp.exp(-a))


def block_kernel(
    noisy, cot, mixing, film, embed, kern,
    out_o, gn_o, gm_o, gat_o,
    npad, nlo, nhi, normed, rinv, ga, ca, mx,
    psend, precv, pown, osend, orecv, ocore, oown,
    gms, yr, ys, zr, zs,
    gs, gkacc, sm, smq, smx, smr, smt,
    ssem, rsem, lsem,
):
    me = Places()

    @pl.loop(0, BAND // ROWS)
    def _(r):
        base = pl.multiple_of(r * ROWS, ROWS)
        for t in range(NT):
            npad[t, pl.ds(base + 8, ROWS), :] = noisy[t, pl.ds(base, ROWS), :].astype(F32)

    barrier = pltpu.get_barrier_semaphore()
    peers = [f(k) for f in (me.q, me.xp, me.yp, me.zp) for k in (1, 2, 3)]
    for peer in peers + [me.nb(1), me.nb(-1), me.zo(2), me.zo(3)]:
        pl.semaphore_signal(barrier, inc=1, device_id=peer, device_id_type=MESH)
    pl.semaphore_wait(barrier, len(peers) + 4)

    copies = []

    def rcopy(src, dst, dev):
        i = len(copies)
        copy = pltpu.make_async_remote_copy(
            src_ref=src, dst_ref=dst, send_sem=ssem.at[i], recv_sem=rsem.at[i],
            device_id=dev, device_id_type=MESH,
        )
        copies.append(copy)
        copy.start()
        return copy

    def arrive(group):
        for copy in group:
            copy.wait_recv()

    halo_in = [
        rcopy(noisy.at[:, pl.ds(0, 16), :], nhi, me.nb(-1)),
        rcopy(noisy.at[:, pl.ds(BAND - 16, 16), :], nlo, me.nb(1)),
    ]

    def ca_slot(k, t):
        return ca.at[t, pl.ds(k * BAND, BAND), :]

    cot_z = [rcopy(cot.at[t], ca_slot(2, t), me.q(2)) for t in range(NT)]
    cot_c = [rcopy(cot.at[t], ca_slot(1, t), me.q(1)) for t in range(NT)]

    def mix_cols(k, j):
        zl, c = me.qpos(k)
        band = zl * 8 + ((me.x + j) % 4) * 2 + c
        return mixing.at[:, pl.ds(pl.multiple_of(band * BAND, BAND), BAND)]

    def mix_slot(k, j):
        return mx.at[pl.ds(k * BAND, BAND), pl.ds(j * BAND, BAND)]

    local = []
    mix_in = {}
    for j in (2, 1, 3, 0):
        mix_in[j] = [
            rcopy(mix_cols(k, j), mix_slot(k, j), me.q(k) if k == 1 else me.zo(k))
            for k in (1, 2, 3)
        ]
        local.append(pltpu.make_async_copy(mix_cols(0, j), mix_slot(0, j), lsem.at[j]))
    for t in range(NT):
        local.append(pltpu.make_async_copy(cot.at[t], ca_slot(0, t), lsem.at[4 + t]))
    for copy in local:
        copy.start()

    arrive(halo_in)
    low_on = jnp.where(me.fr > 0, 1.0, 0.0).astype(F32)
    high_on = jnp.where(me.fr < 15, 1.0, 0.0).astype(F32)
    for t in range(NT):
        npad[t, 0:8, :] = nlo[t].astype(F32)[8:16] * low_on
        npad[t, BAND + 8 : BAND + 16, :] = nhi[t].astype(F32)[0:8] * high_on

    scale1 = film[0:1, :]
    shift = film[1:2, :]

    def noisy_windows(base):
        wins = []
        for t in range(NT):
            w = npad[t, pl.ds(base, ROWS + 16), :]
            wins.append([w[7 + i : 7 + i + ROWS] for i in range(3)])
        return wins

    def forward_rows(r):
        base = pl.multiple_of(r * ROWS, ROWS)
        wins = noisy_windows(base)
        for t in range(NT):
            st = None
            for tp in range(NT):
                for i in range(3):
                    term = kern[i * 3 + tp - t + 1][None, :] * wins[tp][i]
                    st = term if st is None else st + term
            ri = lax.rsqrt(jnp.mean(st * st, axis=-1, keepdims=True) + 1e-05)
            nm = st * ri
            normed[t, pl.ds(base, ROWS), :] = nm
            rinv[t, pl.ds(base, ROWS), :] = jnp.broadcast_to(ri, (ROWS, 128))
            act = nm * scale1 + shift
            ga[t, pl.ds(base, ROWS), :] = (act * sigmoid(act)).astype(BF16)

    half = BAND // 2

    def gate_rows(slot, h):
        return ga.at[:, pl.ds(slot * BAND + h * half, half), :]

    gate_in = {}
    for h in range(2):
        pl.loop(h * half // ROWS, (h + 1) * half // ROWS)(forward_rows)
        gate_in[3, h] = rcopy(gate_rows(0, h), gate_rows(3, h), me.xp(1))
        gate_in[1, h] = rcopy(gate_rows(0, h), gate_rows(1, h), me.xp(3))

    def mixing_grad(j):
        acc = None
        for t in range(NT):
            part = lax.dot_general(
                ca[t], ga[t, pl.ds(j * BAND, BAND), :],
                (((1,), (1,)), ((), ())), preferred_element_type=F32,
            )
            acc = part if acc is None else acc + part
        gms[j] = acc.astype(BF16).reshape(4, BAND, BAND)
        sent = []
        for m in (2, 1, 3):
            y2 = (me.y + m) % 4
            rows = pl.ds(pl.multiple_of(y2 * 64, 64), 64)
            sent.append(rcopy(gms.at[j, :, rows, :], yr.at[j, m - 1], me.yp(m)))
        return sent

    def gate_grad(j):
        mt = mx[:, pl.ds(j * BAND, BAND)].T
        return [jnp.dot(mt, ca[t], preferred_element_type=F32) for t in range(NT)]

    def mixed(k, t):
        return jnp.dot(mx[pl.ds(k * BAND, BAND), :], ga[t], preferred_element_type=F32)

    yrows = pl.ds(pl.multiple_of(me.y * 64, 64), 64)
    zrows = pl.ds(pl.multiple_of(me.zh * 16, 16), 16)
    mine = pl.ds(pl.multiple_of(me.y * 64 + me.zh * 16, 16), 16)

    def y_sum(j):
        arrive(y_in[j])
        for k in range(4):
            total = gms[j, k, yrows, :].astype(F32)
            for m in range(3):
                total = total + yr[j, m, k].astype(F32)
            ys[j, k] = total.astype(BF16)
        sent = []
        for m in (2, 1, 3):
            z2 = (me.zh + m) % 4
            rows = pl.ds(pl.multiple_of(z2 * 16, 16), 16)
            sent.append(rcopy(ys.at[j, :, rows, :], zr.at[j, m - 1], me.zp(m)))
        z_in[j] = sent

    def z_sum(j):
        arrive(z_in[j])
        for k in range(4):
            total = ys[j, k, zrows, :].astype(F32)
            for m in range(3):
                total = total + zr[j, m, k].astype(F32)
            if k == 0:
                gm_o[j, mine, pl.ds(0, BAND)] = total.astype(BF16)
            else:
                zs[j, k - 1] = total.astype(BF16)
        f_in[j] = [
            rcopy(zs.at[j, k - 1], gm_o.at[j, mine, pl.ds(k * BAND, BAND)], me.q(k))
            for k in (2, 3, 1)
        ]

    def z_gather(j):
        arrive(f_in[j])
        az_in[j] = [rcopy(gm_o.at[j, mine], gm_o.at[j, mine], me.zp(m)) for m in (2, 1, 3)]

    def y_gather(j):
        arrive(az_in[j])
        ay_in[j] = [rcopy(gm_o.at[j, yrows], gm_o.at[j, yrows], me.yp(m)) for m in (2, 1, 3)]

    y_in, z_in, f_in, az_in, ay_in = {}, {}, {}, {}, {}

    cot_f = []

    def cot_pass(t):
        arrive([cot_z[t]])
        cot_f.append(rcopy(ca_slot(2, t), ca_slot(3, t), me.q(1)))

    cot_pass(0)
    arrive([gate_in[3, 0]])
    gate_in[2, 0] = rcopy(gate_rows(3, 0), gate_rows(2, 0), me.xp(1))
    cot_pass(1)
    arrive(cot_c + cot_f)
    for copy in local:
        copy.wait()
    y_in[0] = mixing_grad(0)

    def gate_part(j):
        arrive(mix_in[j])
        parts = gate_grad(j)
        for t in range(NT):
            psend[j - 1, t] = parts[t].astype(BF16)

    def gate_send(j):
        return rcopy(psend.at[j - 1], precv.at[j - 1], me.xp(j))

    gate_part(2)
    arrive([gate_in[1, 1]])
    gate_in[2, 1] = rcopy(gate_rows(1, 1), gate_rows(2, 1), me.xp(3))
    p_in = [gate_send(2)]
    arrive([gate_in[3, 1]])
    y_in[3] = mixing_grad(3)
    arrive([gate_in[1, 0]])
    y_in[1] = mixing_grad(1)
    for j in (1, 3):
        gate_part(j)
        p_in.append(gate_send(j))
    y_sum(0)
    arrive([gate_in[2, 0], gate_in[2, 1]])
    y_in[2] = mixing_grad(2)
    arrive(mix_in[0])
    for t in range(NT):
        osend[2, t] = mixed(3, t).astype(BF16)
    oc_in = rcopy(osend.at[2], ocore, me.q(1))
    for t in range(NT):
        osend[0, t] = mixed(1, t).astype(BF16)
    o_in = [rcopy(osend.at[0], orecv.at[0], me.q(1))]
    arrive([oc_in])
    for t in range(NT):
        osend[1, t] = (mixed(2, t) + ocore[t].astype(F32)).astype(BF16)
    o_in.append(rcopy(osend.at[1], orecv.at[1], me.q(2)))
    z_sum(0)
    y_sum(3)
    parts = gate_grad(0)
    for t in range(NT):
        pown[t] = parts[t]
    z_gather(0)
    for t in range(NT):
        oown[t] = mixed(0, t)
    y_sum(1)
    z_sum(3)
    y_gather(0)
    z_gather(3)
    z_sum(1)
    y_sum(2)
    y_gather(3)
    z_gather(1)

    arrive(o_in)

    @pl.loop(0, BAND // ROWS)
    def _(r):
        rows = pl.ds(pl.multiple_of(r * ROWS, ROWS), ROWS)
        for t in range(NT):
            total = oown[t, rows, :] + noisy[t, rows, :].astype(F32)
            for m in range(2):
                total = total + orecv[m, t, rows, :].astype(F32)
            out_o[t, rows, :] = total.astype(BF16)

    z_sum(2)
    y_gather(1)

    arrive(p_in)
    gkacc[...] = jnp.zeros_like(gkacc)

    @pl.loop(0, BAND // ROWS)
    def _(r):
        base = pl.multiple_of(r * ROWS, ROWS)
        rows = pl.ds(base, ROWS)
        wins = noisy_windows(base)
        for t in range(NT):
            gg = pown[t, rows, :]
            for m in range(3):
                gg = gg + precv[m, t, rows, :].astype(F32)
            nm = normed[t, rows, :]
            ri = rinv[t, rows, :][:, 0:1]
            act = nm * scale1 + shift
            sig = sigmoid(act)
            gact = gg * sig * (1.0 + act * (1.0 - sig))
            prod = gact * nm
            gkacc[9] += prod[0:8] + prod[8:16]
            gkacc[10] += gact[0:8] + gact[8:16]
            gnm = gact * scale1
            mean = jnp.mean(gnm * nm, axis=-1, keepdims=True)
            gst = ri * (gnm - nm * mean)
            gs[t, pl.ds(base + 8, ROWS), :] = gst
            for tp in range(NT):
                for i in range(3):
                    prod = wins[tp][i] * gst
                    gkacc[i * 3 + tp - t + 1] += prod[0:8] + prod[8:16]

    halo_gs = [
        rcopy(gs.at[:, pl.ds(8, 8), :], gs.at[:, pl.ds(BAND + 8, 8), :], me.nb(-1)),
        rcopy(gs.at[:, pl.ds(BAND, 8), :], gs.at[:, pl.ds(0, 8), :], me.nb(1)),
    ]
    sm[...] = jnp.zeros_like(sm)
    for i in range(11):
        sm[i : i + 1, :] = jnp.sum(gkacc[i], axis=0, keepdims=True)
    smq_in = [rcopy(sm, smq.at[k - 1], me.q(k)) for k in (2, 3, 1)]
    z_gather(2)
    arrive(smq_in)
    smt[...] = sm[...] + smq[0] + smq[1] + smq[2]
    smx_in = [rcopy(smt, smx.at[k - 1], me.xp(k)) for k in (2, 1, 3)]

    for copy in halo_gs:
        copy.wait()
    for t in range(NT):
        gs[t, 0:8, :] = gs[t, 0:8, :] * low_on
        gs[t, BAND + 8 : BAND + 16, :] = gs[t, BAND + 8 : BAND + 16, :] * high_on

    @pl.loop(0, BAND // ROWS)
    def _(r):
        base = pl.multiple_of(r * ROWS, ROWS)
        rows = pl.ds(base, ROWS)
        wins = []
        for t in range(NT):
            w = gs[t, pl.ds(base, ROWS + 16), :]
            wins.append([w[9 - i : 9 - i + ROWS] for i in range(3)])
        for tp in range(NT):
            back = cot[tp, rows, :].astype(F32)
            for t in range(NT):
                for i in range(3):
                    back = back + kern[i * 3 + tp - t + 1][None, :] * wins[t][i]
            gn_o[tp, rows, :] = back.astype(BF16)

    arrive(smx_in)
    smr[...] = smt[...] + smx[0] + smx[1] + smx[2]
    smr[11:12, :] = embed[0:1, :]
    gat_o[me.dp] = smr[...]
    gy_in = [rcopy(smr, gat_o.at[me.dp], me.yp(m)) for m in (2, 1, 3)]
    y_gather(2)
    arrive(gy_in)
    four = pl.ds(me.zh * 4, 4)
    gz_in = [rcopy(gat_o.at[four], gat_o.at[four], me.zp(m)) for m in (2, 1, 3)]
    for j in (0, 3, 1, 2):
        arrive(ay_in[j])
    arrive(gz_in)
    done = set(id(copy) for copy in halo_gs)
    for copy in copies:
        if id(copy) not in done:
            copy.wait_send()


N_COPIES = 2 + 6 + 12 + 6 + 3 + 3 + 12 * 5 + 2 + 12


def fused_block(noisy, cot, mixing, film, embed, kern):
    vmem = pl.BlockSpec(memory_space=pltpu.VMEM)
    hbm = pl.BlockSpec(memory_space=pl.ANY)
    act = (NT, BAND, C)
    full = (NT, 4 * BAND, C)
    pad = (NT, BAND + 16, C)
    return pl.pallas_call(
        block_kernel,
        out_shape=(
            jax.ShapeDtypeStruct(act, BF16),
            jax.ShapeDtypeStruct(act, BF16),
            jax.ShapeDtypeStruct((4, BAND, 4 * BAND), BF16),
            jax.ShapeDtypeStruct((16, 16, C), F32),
        ),
        in_specs=[vmem, vmem, hbm, vmem, vmem, vmem],
        out_specs=(vmem, vmem, vmem, vmem),
        scratch_shapes=[
            pltpu.VMEM(pad, F32),
            pltpu.VMEM((NT, 16, C), BF16),
            pltpu.VMEM((NT, 16, C), BF16),
            pltpu.VMEM(act, F32),
            pltpu.VMEM((NT, BAND, 128), F32),
            pltpu.VMEM(full, BF16),
            pltpu.VMEM(full, BF16),
            pltpu.VMEM((4 * BAND, 4 * BAND), BF16),
            pltpu.VMEM((3,) + act, BF16),
            pltpu.VMEM((3,) + act, BF16),
            pltpu.VMEM(act, F32),
            pltpu.VMEM((3,) + act, BF16),
            pltpu.VMEM((2,) + act, BF16),
            pltpu.VMEM(act, BF16),
            pltpu.VMEM(act, F32),
            pltpu.VMEM((4, 4, BAND, BAND), BF16),
            pltpu.VMEM((4, 3, 4, 64, BAND), BF16),
            pltpu.VMEM((4, 4, 64, BAND), BF16),
            pltpu.VMEM((4, 3, 4, 16, BAND), BF16),
            pltpu.VMEM((4, 3, 16, BAND), BF16),
            pltpu.VMEM(pad, F32),
            pltpu.VMEM((11, 8, C), F32),
            pltpu.VMEM((16, C), F32),
            pltpu.VMEM((3, 16, C), F32),
            pltpu.VMEM((3, 16, C), F32),
            pltpu.VMEM((16, C), F32),
            pltpu.VMEM((16, C), F32),
            pltpu.SemaphoreType.DMA((N_COPIES,)),
            pltpu.SemaphoreType.DMA((N_COPIES,)),
            pltpu.SemaphoreType.DMA((6,)),
        ],
        compiler_params=pltpu.CompilerParams(
            collective_id=0, has_side_effects=True, vmem_limit_bytes=60 * 1024 * 1024
        ),
    )(noisy, cot, mixing, film, embed, kern)


def finish_kernel(out, gn, gm, gat, out_o, gn_o, gm_o, gk_o, film_o):
    step = pl.program_id(0)
    fr = lax.axis_index("freq")
    zl, x, c = fr // 8, (fr // 2) % 4, fr % 2
    for src, dst in ((out, out_o), (gn, gn_o)):
        dst[...] = jnp.stack([src[t].astype(F32) for t in range(NT)], axis=1).astype(BF16)
    for k in range(4):
        bz = zl if k < 2 else 1 - zl
        bc = c if k % 2 == 0 else 1 - c
        for j in range(4):
            band = bz * 8 + ((x + j) % 4) * 2 + bc
            cols = pl.ds(pl.multiple_of(band * BAND, BAND), BAND)
            gm_o[:, cols] = gm[j, :, k * BAND : (k + 1) * BAND].astype(F32)
    wide = film_o.shape[0]
    embeds = gat[:, 11, pl.ds(pl.multiple_of(step * wide, wide), wide)]
    both = jnp.concatenate([gat[:, 9, :], gat[:, 10, :]], axis=1)
    film_o[...] = lax.dot_general(
        embeds, both, (((0,), (0,)), ((), ())),
        preferred_element_type=F32, precision=lax.Precision.HIGHEST,
    )

    @pl.when(step == 0)
    def _():
        gk_o[...] = jnp.sum(gat[:, 0:9, :], axis=0)


def finish(out, grad_noisy, grad_mixing, gathered):
    steps = 4
    rows, wide = BAND // steps, C // steps
    planes = pl.BlockSpec((NT, rows, C), lambda i: (0, i, 0))
    pairs = pl.BlockSpec((rows, NT, C), lambda i: (i, 0, 0))
    return pl.pallas_call(
        finish_kernel,
        grid=(steps,),
        out_shape=(
            jax.ShapeDtypeStruct((BAND, NT, C), BF16),
            jax.ShapeDtypeStruct((BAND, NT, C), BF16),
            jax.ShapeDtypeStruct((BAND, 16 * BAND), F32),
            jax.ShapeDtypeStruct((9, C), F32),
            jax.ShapeDtypeStruct((C, 2 * C), F32),
        ),
        in_specs=[
            planes,
            planes,
            pl.BlockSpec((4, rows, 4 * BAND), lambda i: (0, i, 0)),
            pl.BlockSpec((16, 16, C), lambda i: (0, 0, 0)),
        ],
        out_specs=(
            pairs,
            pairs,
            pl.BlockSpec((rows, 16 * BAND), lambda i: (i, 0)),
            pl.BlockSpec((9, C), lambda i: (0, 0)),
            pl.BlockSpec((wide, 2 * C), lambda i: (i, 0)),
        ),
        compiler_params=pltpu.CompilerParams(vmem_limit_bytes=24 * 1024 * 1024),
    )(out, grad_noisy, grad_mixing, gathered)


def embed_steps(timestep, width):
    half = width // 2
    freqs = jnp.exp(-math.log(10000.0) * jnp.arange(half, dtype=jnp.float32) / half)
    angles = timestep.astype(jnp.float32)[:, None] * freqs[None, :]
    return jnp.concatenate([jnp.sin(angles), jnp.cos(angles)], axis=1).astype(jnp.bfloat16)


def on_device(noisy, timestep, kernel, film_weight, mixing, cotangent):
    embed = embed_steps(timestep, C)
    film = jnp.dot(embed, film_weight, preferred_element_type=jnp.float32)
    film = jnp.concatenate([1.0 + film[:, :C], film[:, C:]], axis=0)
    planes = [jnp.transpose(a[0], (1, 0, 2)) for a in (noisy, cotangent)]
    out, grad_noisy, grad_mixing, gathered = fused_block(
        planes[0], planes[1], mixing, film, embed.astype(F32), kernel.reshape(9, C)
    )
    output, grad_noisy, grad_mixing, grad_kernel, grad_film = finish(
        out, grad_noisy, grad_mixing, gathered
    )
    grad_kernel = grad_kernel.reshape(3, 3, C)
    output, grad_noisy = output[None], grad_noisy[None]
    return (output, grad_noisy, grad_mixing, grad_kernel, grad_film)


def solution(mesh):
    return jax.shard_map(
        on_device,
        mesh=mesh,
        in_specs=(
            P("dp", "freq", None, None),
            P("dp"),
            P(),
            P(),
            P("freq", None),
            P("dp", "freq", None, None),
        ),
        out_specs=(
            P("dp", "freq", None, None),
            P("dp", "freq", None, None),
            P("freq", None),
            P(),
            P(),
        ),
        check_vma=False,
    )
```

```python
import functools
import math

import jax
import jax.numpy as jnp
from jax import lax
from jax.experimental import pallas as pl
from jax.experimental.pallas import tpu as pltpu
from jax.sharding import PartitionSpec as P

MESH = pl.DeviceIdType.MESH
BAND = 256
C = 512
NT = 2
ROWS = 16
F32 = jnp.float32
BF16 = jnp.bfloat16


class Places:
    def __init__(self):
        self.dp = lax.axis_index("dp")
        self.fr = lax.axis_index("freq")
        self.zh, self.y = self.dp // 4, self.dp % 4
        self.zl, self.x, self.c = self.fr // 8, (self.fr // 2) % 4, self.fr % 2

    def qpos(self, k):
        zl = self.zl if k < 2 else 1 - self.zl
        c = self.c if k % 2 == 0 else 1 - self.c
        return zl, c

    def q(self, k):
        zl, c = self.qpos(k)
        return (self.dp, zl * 8 + self.x * 2 + c)

    def xp(self, k):
        return (self.dp, self.zl * 8 + ((self.x + k) % 4) * 2 + self.c)

    def yp(self, k):
        return (self.zh * 4 + (self.y + k) % 4, self.fr)

    def zp(self, k):
        return (((self.zh + k) % 4) * 4 + self.y, self.fr)

    def zo(self, k):
        zl, c = self.qpos(k)
        zh = (self.zh + jnp.where(self.zl == 1, 1, 3)) % 4
        return (zh * 4 + self.y, zl * 8 + self.x * 2 + c)

    def band(self, d):
        return (self.dp, (self.fr + 16 + d) % 16)


def sigmoid(a):
    return 1.0 / (1.0 + jnp.exp(-a))


def block_kernel(
    noisy, cot, mixing, film, embed, kern,
    out_o, gn_o, gm_o, gat_o, eg_o,
    npad, nlo, nhi, normed, rinv, ga, ca, mx,
    psend, pmid, precv, pown, osend, orecv, ocore, oown,
    gms, ymid, yout, yr, ys, zr, zs,
    gs, gkacc, sm, smq, smx, smr, smt, smy, smz,
    ssem, rsem, lsem, order,
):
    me = Places()
    half = BAND // 2
    scale1 = film[0:1, :]
    shift = film[1:2, :]
    low_on = jnp.where(me.fr > 0, 1.0, 0.0).astype(F32)
    high_on = jnp.where(me.fr < 15, 1.0, 0.0).astype(F32)
    yrows = pl.ds(pl.multiple_of(me.y * 64, 64), 64)
    zrows = pl.ds(pl.multiple_of(me.zh * 16, 16), 16)
    mine = pl.ds(pl.multiple_of(me.y * 64 + me.zh * 16, 16), 16)
    four = pl.ds(me.zh * 4, 4)
    sent = []
    groups = {}

    def send(group, src, dst, dev):
        i = len(sent)
        copy = pltpu.make_async_remote_copy(
            src_ref=src, dst_ref=dst, send_sem=ssem.at[i], recv_sem=rsem.at[i],
            device_id=dev, device_id_type=MESH,
        )
        sent.append(copy)
        groups.setdefault(group, []).append(copy)
        copy.start()

    def arrive(*names):
        for name in names:
            for copy in groups.pop(name, []):
                copy.wait_recv()

    def all_sent():
        while sent_open := [i for i in range(len(sent)) if i not in drained]:
            for i in sent_open:
                sent[i].wait_send()
                drained.add(i)

    drained = set()
    local = {}

    def rows_loop(first, last):
        return pl.loop(first // ROWS, last // ROWS)

    def pad():
        @rows_loop(0, BAND)
        def _(r):
            base = pl.multiple_of(r * ROWS, ROWS)
            for t in range(NT):
                npad[t, pl.ds(base + 8, ROWS), :] = noisy[t, pl.ds(base, ROWS), :].astype(F32)

    barrier = pltpu.get_barrier_semaphore()
    greeted = [f(k) for f in (me.q, me.xp, me.yp, me.zp) for k in (1, 2, 3)]
    greeted += [me.band(1), me.band(-1), me.zo(2), me.zo(3)]

    def greet():
        for peer in greeted:
            pl.semaphore_signal(barrier, inc=1, device_id=peer, device_id_type=MESH)

    def enter():
        pl.semaphore_wait(barrier, len(greeted))

    def halo():
        send("halo", noisy.at[:, pl.ds(0, 16), :], nhi, me.band(-1))
        send("halo", noisy.at[:, pl.ds(BAND - 16, 16), :], nlo, me.band(1))

    def ca_slot(k, t):
        return ca.at[t, pl.ds(k * BAND, BAND), :]

    def cots():
        for t in range(NT):
            send(f"cotz{t}", cot.at[t], ca_slot(2, t), me.q(2))
        for t in range(NT):
            send("cot", cot.at[t], ca_slot(1, t), me.q(1))

    def mix_cols(k, j):
        zl, c = me.qpos(k)
        band = zl * 8 + ((me.x + j) % 4) * 2 + c
        return mixing.at[:, pl.ds(pl.multiple_of(band * BAND, BAND), BAND)]

    def mix_slot(k, j):
        return mx.at[pl.ds(k * BAND, BAND), pl.ds(j * BAND, BAND)]

    def mix():
        for j in (2, 1, 3, 0):
            for k in (1, 2, 3):
                peer = me.q(k) if k == 1 else me.zo(k)
                send(f"mix{j}", mix_cols(k, j), mix_slot(k, j), peer)

    def locals_in():
        for j in range(4):
            local[j] = pltpu.make_async_copy(mix_cols(0, j), mix_slot(0, j), lsem.at[j])
        for t in range(NT):
            local[4 + t] = pltpu.make_async_copy(cot.at[t], ca_slot(0, t), lsem.at[4 + t])
        for copy in local.values():
            copy.start()

    def locals_done():
        for copy in local.values():
            copy.wait()

    def halo_rows():
        arrive("halo")
        for t in range(NT):
            npad[t, 0:8, :] = nlo[t].astype(F32)[8:16] * low_on
            npad[t, BAND + 8 : BAND + 16, :] = nhi[t].astype(F32)[0:8] * high_on

    def noisy_windows(base):
        wins = []
        for t in range(NT):
            w = npad[t, pl.ds(base, ROWS + 16), :]
            wins.append([w[7 + i : 7 + i + ROWS] for i in range(3)])
        return wins

    def gate_rows(slot, first, last):
        return ga.at[:, pl.ds(slot * BAND + first, last - first), :]

    def forward(first, last):
        @rows_loop(first, last)
        def _(r):
            base = pl.multiple_of(r * ROWS, ROWS)
            wins = noisy_windows(base)
            for t in range(NT):
                st = None
                for tp in range(NT):
                    for i in range(3):
                        term = kern[i, tp - t + 1 : tp - t + 2, :] * wins[tp][i]
                        st = term if st is None else st + term
                ri = lax.rsqrt(jnp.mean(st * st, axis=-1, keepdims=True) + 1e-05)
                nm = st * ri
                normed[t, pl.ds(base, ROWS), :] = nm
                rinv[t, pl.ds(base, ROWS), :] = jnp.broadcast_to(ri, (ROWS, 128))
                act = nm * scale1 + shift
                ga[t, pl.ds(base, ROWS), :] = (act * sigmoid(act)).astype(BF16)

    def gate_send(first, last):
        h = first // half
        send(f"ga3{h}", gate_rows(0, first, last), gate_rows(3, first, last), me.xp(1))
        send(f"ga1{h}", gate_rows(0, first, last), gate_rows(1, first, last), me.xp(3))

    def gate_right():
        arrive("ga30")
        send("ga2", gate_rows(3, 0, half), gate_rows(2, 0, half), me.xp(1))

    def gate_left():
        arrive("ga11")
        send("ga2", gate_rows(1, half, BAND), gate_rows(2, half, BAND), me.xp(3))

    def cot_pass(t):
        arrive(f"cotz{t}")
        send("cot", ca_slot(2, t), ca_slot(3, t), me.q(1))

    def cot_done():
        arrive("cot")
        locals_done()

    def gm_product(j):
        arrive(*{0: (), 1: ("ga10", "ga11"), 2: ("ga2",), 3: ("ga30", "ga31")}[j])
        acc = None
        for t in range(NT):
            part = lax.dot_general(
                ca[t], ga[t, pl.ds(j * BAND, BAND), :],
                (((1,), (1,)), ((), ())), preferred_element_type=F32,
            )
            acc = part if acc is None else acc + part
        gms[j] = acc.astype(BF16).reshape(4, BAND, BAND)

    def y_rows(m):
        return pl.ds(pl.multiple_of((me.y + m) % 4 * 64, 64), 64)

    def gm_send(j):
        near, far, back = y_rows(1), y_rows(2), y_rows(3)
        send(f"ya{j}", gms.at[j, pl.ds(0, 2), far, :], ymid.at[j, 0], me.yp(1))
        send(f"yb{j}", gms.at[j, pl.ds(2, 2), far, :], ymid.at[j, 1], me.yp(3))
        send(f"y{j}", gms.at[j, pl.ds(2, 2), near, :], yr.at[j, 0, pl.ds(2, 2)], me.yp(1))
        send(f"y{j}", gms.at[j, pl.ds(0, 2), back, :], yr.at[j, 1, pl.ds(0, 2)], me.yp(3))

    def y_join(j):
        for side, group, rows in ((0, f"ya{j}", y_rows(1)), (1, f"yb{j}", y_rows(3))):
            arrive(group)
            for k in range(2):
                total = gms[j, 2 * side + k, rows, :].astype(F32) + ymid[j, side, k].astype(F32)
                yout[j, side, k] = total.astype(BF16)
            send(
                f"y{j}", yout.at[j, side], yr.at[j, side, pl.ds(2 * side, 2)],
                me.yp(1 if side == 0 else 3),
            )

    def y_sum(j):
        arrive(f"y{j}")
        for k in range(4):
            total = gms[j, k, yrows, :].astype(F32)
            for m in range(2):
                total = total + yr[j, m, k].astype(F32)
            ys[j, k] = total.astype(BF16)
        for m in (2, 1, 3):
            z2 = (me.zh + m) % 4
            rows = pl.ds(pl.multiple_of(z2 * 16, 16), 16)
            send(f"z{j}", ys.at[j, :, rows, :], zr.at[j, m - 1], me.zp(m))

    def z_sum(j):
        arrive(f"z{j}")
        for k in range(4):
            total = ys[j, k, zrows, :].astype(F32)
            for m in range(3):
                total = total + zr[j, m, k].astype(F32)
            if k == 0:
                gm_o[j, mine, pl.ds(0, BAND)] = total.astype(BF16)
            else:
                zs[j, k - 1] = total.astype(BF16)
        for k in (2, 3, 1):
            send(f"f{j}", zs.at[j, k - 1], gm_o.at[j, mine, pl.ds(k * BAND, BAND)], me.q(k))

    def z_gather(j):
        arrive(f"f{j}")
        for m in (2, 1, 3):
            send(f"az{j}", gm_o.at[j, mine], gm_o.at[j, mine], me.zp(m))

    def y_gather(j):
        arrive(f"az{j}")
        send(f"ar{j}", gm_o.at[j, yrows], gm_o.at[j, yrows], me.yp(1))
        send(f"al{j}", gm_o.at[j, yrows], gm_o.at[j, yrows], me.yp(3))

    def y_pass(j):
        for group, m, first, to in ((f"ar{j}", 3, 0, 1), (f"al{j}", 1, 32, 3)):
            arrive(group)
            rows = pl.ds(pl.multiple_of((me.y + m) % 4 * 64 + first, 32), 32)
            send("ay", gm_o.at[j, rows], gm_o.at[j, rows], me.yp(to))

    def gate_grad(j):
        arrive(f"mix{j}")
        mt = mx[:, pl.ds(j * BAND, BAND)].T
        for t in range(NT):
            part = jnp.dot(mt, ca[t], preferred_element_type=F32)
            if j == 0:
                pown[t] = part
            else:
                psend[j - 1, t] = part.astype(BF16)

    def p_far():
        send("pa0", psend.at[1, 0], pmid.at[0], me.xp(1))
        send("pa1", psend.at[1, 1], pmid.at[1], me.xp(3))

    def p_right():
        send("p", psend.at[0, 1], precv.at[0, 1], me.xp(1))

    def p_left():
        send("p", psend.at[2, 0], precv.at[1, 0], me.xp(3))

    def p_join():
        arrive("pa0")
        psend[0, 0] = (psend[0, 0].astype(F32) + pmid[0].astype(F32)).astype(BF16)
        send("p", psend.at[0, 0], precv.at[0, 0], me.xp(1))
        arrive("pa1")
        psend[2, 1] = (psend[2, 1].astype(F32) + pmid[1].astype(F32)).astype(BF16)
        send("p", psend.at[2, 1], precv.at[1, 1], me.xp(3))

    def mixed(k, t):
        return jnp.dot(mx[pl.ds(k * BAND, BAND), :], ga[t], preferred_element_type=F32)

    def mixed_far():
        arrive("ga10", "ga11", "ga2", "ga30", "ga31", "mix0", "mix1", "mix2", "mix3")
        for t in range(NT):
            osend[2, t] = mixed(3, t).astype(BF16)
        send("oc", osend.at[2], ocore, me.q(1))

    def mixed_core():
        for t in range(NT):
            osend[0, t] = mixed(1, t).astype(BF16)
        send("o", osend.at[0], orecv.at[0], me.q(1))

    def mixed_z():
        parts = [mixed(2, t) for t in range(NT)]
        arrive("oc")
        for t in range(NT):
            osend[1, t] = (parts[t] + ocore[t].astype(F32)).astype(BF16)
        send("o", osend.at[1], orecv.at[1], me.q(2))

    def mixed_own():
        for t in range(NT):
            oown[t] = mixed(0, t)

    def output():
        arrive("o")

        @rows_loop(0, BAND)
        def _(r):
            rows = pl.ds(pl.multiple_of(r * ROWS, ROWS), ROWS)
            for t in range(NT):
                total = oown[t, rows, :] + noisy[t, rows, :].astype(F32)
                for m in range(2):
                    total = total + orecv[m, t, rows, :].astype(F32)
                out_o[t, rows, :] = total.astype(BF16)

    def backward():
        arrive("p")
        gkacc[...] = jnp.zeros_like(gkacc)

        @rows_loop(0, BAND)
        def _(r):
            base = pl.multiple_of(r * ROWS, ROWS)
            rows = pl.ds(base, ROWS)
            wins = noisy_windows(base)
            for t in range(NT):
                gg = pown[t, rows, :]
                for m in range(2):
                    gg = gg + precv[m, t, rows, :].astype(F32)
                nm = normed[t, rows, :]
                ri = rinv[t, rows, :][:, 0:1]
                act = nm * scale1 + shift
                sig = sigmoid(act)
                gact = gg * sig * (1.0 + act * (1.0 - sig))
                prod = gact * nm
                gkacc[9] += prod[0:8] + prod[8:16]
                gkacc[10] += gact[0:8] + gact[8:16]
                gnm = gact * scale1
                mean = jnp.mean(gnm * nm, axis=-1, keepdims=True)
                gst = ri * (gnm - nm * mean)
                gs[t, pl.ds(base + 8, ROWS), :] = gst
                for tp in range(NT):
                    for i in range(3):
                        prod = wins[tp][i] * gst
                        gkacc[i * 3 + tp - t + 1] += prod[0:8] + prod[8:16]

    def grad_halo():
        send("gs", gs.at[:, pl.ds(8, 8), :], gs.at[:, pl.ds(BAND + 8, 8), :], me.band(-1))
        send("gs", gs.at[:, pl.ds(BAND, 8), :], gs.at[:, pl.ds(0, 8), :], me.band(1))

    def sums_q():
        sm[...] = jnp.zeros_like(sm)
        for i in range(11):
            sm[i : i + 1, :] = jnp.sum(gkacc[i], axis=0, keepdims=True)
        for k in (2, 3, 1):
            send("smq", sm, smq.at[k - 1], me.q(k))

    def sums_x():
        arrive("smq")
        smt[...] = sm[...] + smq[0] + smq[1] + smq[2]
        for k in (2, 1, 3):
            send("smx", smt, smx.at[k - 1], me.xp(k))

    def sums_y():
        arrive("smx")
        smr[...] = smt[...] + smx[0] + smx[1] + smx[2]
        smy[me.y] = smr[...]
        for m in (2, 1, 3):
            send("gy", smr, smy.at[me.y], me.yp(m))

    def sums_z():
        arrive("gy")
        smz[...] = jnp.zeros_like(smz)
        smz[0:16] = smy[0] + smy[1] + smy[2] + smy[3]
        for y in range(4):
            for i in range(2):
                smz[16 + 4 * i + y : 17 + 4 * i + y, :] = smy[y, 9 + i : 10 + i, :]
        gat_o[me.zh] = smz[...]
        for m in (2, 1, 3):
            send("gz", smz, gat_o.at[me.zh], me.zp(m))

    def embeds_y():
        eg_o[me.dp] = embed[...]
        for m in (2, 1, 3):
            send("ey", embed, eg_o.at[me.dp], me.yp(m))

    def embeds_z():
        arrive("ey")
        for m in (2, 1, 3):
            send("ez", eg_o.at[four], eg_o.at[four], me.zp(m))

    def grad_back():
        arrive("gs")
        for t in range(NT):
            gs[t, 0:8, :] = gs[t, 0:8, :] * low_on
            gs[t, BAND + 8 : BAND + 16, :] = gs[t, BAND + 8 : BAND + 16, :] * high_on

        @rows_loop(0, BAND)
        def _(r):
            base = pl.multiple_of(r * ROWS, ROWS)
            rows = pl.ds(base, ROWS)
            wins = []
            for t in range(NT):
                w = gs[t, pl.ds(base, ROWS + 16), :]
                wins.append([w[9 - i : 9 - i + ROWS] for i in range(3)])
            for tp in range(NT):
                back = cot[tp, rows, :].astype(F32)
                for t in range(NT):
                    for i in range(3):
                        back = back + kern[i, tp - t + 1 : tp - t + 2, :] * wins[t][i]
                gn_o[tp, rows, :] = back.astype(BF16)

    tasks = locals()
    for name, *args in order:
        tasks[name](*args)
    for name in list(groups):
        arrive(name)
    all_sent()


ORDER = (
    ("pad",), ("enter",), ("halo",), ("cots",), ("mix",), ("locals_in",), ("embeds_y",), ("halo_rows",),
    ("forward", 0), ("forward", 1), ("cot_pass", 0), ("gate_right",), ("embeds_z",), ("cot_pass", 1),
    ("cot_done",), ("gm_product", 0), ("gm_send", 0), ("gate_grad", 2), ("gate_left",),
    ("gate_send", 2), ("gm_product", 3), ("gm_send", 3), ("gm_product", 1), ("gm_send", 1),
    ("gate_grad", 1), ("gate_send", 1), ("gate_grad", 3), ("gate_send", 3), ("y_sum", 0),
    ("gm_product", 2), ("gm_send", 2), ("mixed_far",), ("mixed_core",), ("mixed_z",),
    ("z_sum", 0), ("y_sum", 3), ("gate_grad", 0), ("z_gather", 0), ("mixed_own",), ("y_sum", 1),
    ("z_sum", 3), ("y_gather", 0), ("z_gather", 3), ("z_sum", 1), ("y_sum", 2), ("y_gather", 3),
    ("z_gather", 1), ("output",), ("z_sum", 2), ("y_gather", 1), ("backward",), ("grad_halo",),
    ("sums_q",), ("z_gather", 2), ("sums_x",), ("grad_back",), ("sums_y",), ("y_gather", 2),
    ("sums_z",),
)
N_COPIES = 2 + 6 + 12 + 10 + 6 + 3 + 4 * (6 + 9 + 4) + 2 + 12 + 6

ORDER = (
    ("pad",), ("greet",), ("forward", 16, 240), ("enter",), ("halo",), ("gate_send", 16, 128),
    ("gate_send", 128, 240), ("cots",), ("mix",), ("locals_in",), ("embeds_y",), ("halo_rows",),
    ("forward", 0, 16), ("forward", 240, 256), ("gate_send", 0, 16), ("gate_send", 240, 256),
    ("cot_pass", 0), ("embeds_z",), ("gate_right",), ("cot_pass", 1), ("cot_done",),
    ("gm_product", 0), ("gm_send", 0), ("gate_grad", 2), ("gate_left",), ("p_far",),
    ("gm_product", 3), ("gm_send", 3), ("gm_product", 1), ("gm_send", 1), ("y_join", 0),
    ("gate_grad", 1), ("p_right",), ("gate_grad", 3), ("p_left",), ("y_join", 3), ("y_sum", 0),
    ("gm_product", 2), ("gm_send", 2), ("y_join", 1), ("p_join",), ("gate_grad", 0),
    ("z_sum", 0), ("y_sum", 3), ("y_join", 2), ("mixed_far",), ("y_sum", 1), ("z_gather", 0),
    ("z_sum", 3), ("mixed_core",), ("y_sum", 2), ("mixed_own",), ("y_gather", 0),
    ("z_gather", 3), ("z_sum", 1), ("y_gather", 3), ("z_gather", 1), ("z_sum", 2), ("y_pass", 0),
    ("backward",), ("grad_halo",), ("sums_q",), ("z_gather", 2), ("y_gather", 1), ("y_pass", 3),
    ("mixed_z",), ("sums_x",), ("y_gather", 2), ("y_pass", 1), ("grad_back",), ("sums_y",),
    ("y_pass", 2), ("sums_z",), ("output",),
)


def fused_block(noisy, cot, mixing, film, embed, kern, order=ORDER, number=0):
    vmem = pl.BlockSpec(memory_space=pltpu.VMEM)
    hbm = pl.BlockSpec(memory_space=pl.ANY)
    act = (NT, BAND, C)
    full = (NT, 4 * BAND, C)
    pad = (NT, BAND + 16, C)
    return pl.pallas_call(
        functools.partial(block_kernel, order=order),
        out_shape=(
            jax.ShapeDtypeStruct(act, BF16),
            jax.ShapeDtypeStruct(act, BF16),
            jax.ShapeDtypeStruct((4, BAND, 4 * BAND), BF16),
            jax.ShapeDtypeStruct((4, 24, C), F32),
            jax.ShapeDtypeStruct((16, 1, C), F32),
        ),
        in_specs=[vmem, vmem, hbm, vmem, vmem, vmem],
        out_specs=(vmem,) * 5,
        scratch_shapes=[
            pltpu.VMEM(pad, F32),
            pltpu.VMEM((NT, 16, C), BF16),
            pltpu.VMEM((NT, 16, C), BF16),
            pltpu.VMEM(act, F32),
            pltpu.VMEM((NT, BAND, 128), F32),
            pltpu.VMEM(full, BF16),
            pltpu.VMEM(full, BF16),
            pltpu.VMEM((4 * BAND, 4 * BAND), BF16),
            pltpu.VMEM((3,) + act, BF16),
            pltpu.VMEM(act, BF16),
            pltpu.VMEM((2,) + act, BF16),
            pltpu.VMEM(act, F32),
            pltpu.VMEM((3,) + act, BF16),
            pltpu.VMEM((2,) + act, BF16),
            pltpu.VMEM(act, BF16),
            pltpu.VMEM(act, F32),
            pltpu.VMEM((4, 4, BAND, BAND), BF16),
            pltpu.VMEM((4, 2, 2, 64, BAND), BF16),
            pltpu.VMEM((4, 2, 2, 64, BAND), BF16),
            pltpu.VMEM((4, 2, 4, 64, BAND), BF16),
            pltpu.VMEM((4, 4, 64, BAND), BF16),
            pltpu.VMEM((4, 3, 4, 16, BAND), BF16),
            pltpu.VMEM((4, 3, 16, BAND), BF16),
            pltpu.VMEM(pad, F32),
            pltpu.VMEM((11, 8, C), F32),
            pltpu.VMEM((16, C), F32),
            pltpu.VMEM((3, 16, C), F32),
            pltpu.VMEM((3, 16, C), F32),
            pltpu.VMEM((16, C), F32),
            pltpu.VMEM((16, C), F32),
            pltpu.VMEM((4, 16, C), F32),
            pltpu.VMEM((24, C), F32),
            pltpu.SemaphoreType.DMA((N_COPIES,)),
            pltpu.SemaphoreType.DMA((N_COPIES,)),
            pltpu.SemaphoreType.DMA((6,)),
        ],
        compiler_params=pltpu.CompilerParams(
            collective_id=number, has_side_effects=True, vmem_limit_bytes=60 * 1024 * 1024
        ),
    )(noisy, cot, mixing, film, embed, kern)


def finish_kernel(out, gn, gm, gat, eg, out_o, gn_o, gm_o, gk_o, film_o):
    step = pl.program_id(0)
    fr = lax.axis_index("freq")
    zl, x, c = fr // 8, (fr // 2) % 4, fr % 2
    for src, dst in ((out, out_o), (gn, gn_o)):
        dst[...] = jnp.stack([src[t].astype(F32) for t in range(NT)], axis=1).astype(BF16)
    for k in range(4):
        bz = zl if k < 2 else 1 - zl
        bc = c if k % 2 == 0 else 1 - c
        for j in range(4):
            band = bz * 8 + ((x + j) % 4) * 2 + bc
            cols = pl.ds(pl.multiple_of(band * BAND, BAND), BAND)
            gm_o[:, cols] = gm[j, :, k * BAND : (k + 1) * BAND].astype(F32)
    wide = film_o.shape[0]
    embeds = eg[:, 0, pl.ds(pl.multiple_of(step * wide, wide), wide)]
    both = jnp.concatenate(
        [jnp.concatenate([gat[z, 16 + 4 * i : 20 + 4 * i] for z in range(4)]) for i in range(2)],
        axis=1,
    )
    film_o[...] = lax.dot_general(
        embeds, both, (((0,), (0,)), ((), ())),
        preferred_element_type=F32, precision=lax.Precision.HIGHEST,
    )

    @pl.when(step == 0)
    def _():
        total = jnp.sum(gat[:, 0:9, :], axis=0)
        for i in range(3):
            gk_o[i] = total[3 * i : 3 * i + 3]


def finish(out, grad_noisy, grad_mixing, sums, embeds):
    steps = 4
    rows, wide = BAND // steps, C // steps
    planes = pl.BlockSpec((NT, rows, C), lambda i: (0, i, 0))
    pairs = pl.BlockSpec((rows, NT, C), lambda i: (i, 0, 0))
    return pl.pallas_call(
        finish_kernel,
        grid=(steps,),
        out_shape=(
            jax.ShapeDtypeStruct((BAND, NT, C), BF16),
            jax.ShapeDtypeStruct((BAND, NT, C), BF16),
            jax.ShapeDtypeStruct((BAND, 16 * BAND), F32),
            jax.ShapeDtypeStruct((3, 3, C), F32),
            jax.ShapeDtypeStruct((C, 2 * C), F32),
        ),
        in_specs=[
            planes,
            planes,
            pl.BlockSpec((4, rows, 4 * BAND), lambda i: (0, i, 0)),
            pl.BlockSpec((4, 24, C), lambda i: (0, 0, 0)),
            pl.BlockSpec((16, 1, C), lambda i: (0, 0, 0)),
        ],
        out_specs=(
            pairs,
            pairs,
            pl.BlockSpec((rows, 16 * BAND), lambda i: (i, 0)),
            pl.BlockSpec((3, 3, C), lambda i: (0, 0, 0)),
            pl.BlockSpec((wide, 2 * C), lambda i: (i, 0)),
        ),
        compiler_params=pltpu.CompilerParams(vmem_limit_bytes=60 * 1024 * 1024),
    )(out, grad_noisy, grad_mixing, sums, embeds)


def embed_steps(timestep, width):
    half = width // 2
    freqs = jnp.exp(-math.log(10000.0) * jnp.arange(half, dtype=jnp.float32) / half)
    angles = timestep.astype(jnp.float32)[:, None] * freqs[None, :]
    return jnp.concatenate([jnp.sin(angles), jnp.cos(angles)], axis=1).astype(jnp.bfloat16)


def on_device(noisy, timestep, kernel, film_weight, mixing, cotangent):
    embed = embed_steps(timestep, C)
    film = jnp.dot(embed, film_weight, preferred_element_type=jnp.float32)
    film = jnp.concatenate([1.0 + film[:, :C], film[:, C:]], axis=0)
    planes = [jnp.transpose(a[0], (1, 0, 2)) for a in (noisy, cotangent)]
    out, grad_noisy, grad_mixing, sums, embeds = fused_block(
        planes[0], planes[1], mixing, film, embed.astype(F32), kernel
    )
    output, grad_noisy, grad_mixing, grad_kernel, grad_film = finish(
        out, grad_noisy, grad_mixing, sums, embeds
    )
    output, grad_noisy = output[None], grad_noisy[None]
    return (output, grad_noisy, grad_mixing, grad_kernel, grad_film)


def solution(mesh):
    return jax.shard_map(
        on_device,
        mesh=mesh,
        in_specs=(
            P("dp", "freq", None, None),
            P("dp"),
            P(),
            P(),
            P("freq", None),
            P("dp", "freq", None, None),
        ),
        out_specs=(
            P("dp", "freq", None, None),
            P("dp", "freq", None, None),
            P("freq", None),
            P(),
            P(),
        ),
        check_vma=False,
    )
```

```python
import functools
import math
import types

import jax
import jax.numpy as jnp
from jax import lax
from jax.experimental import pallas as pl
from jax.experimental.pallas import tpu as pltpu
from jax.sharding import PartitionSpec as P

MESH = pl.DeviceIdType.MESH
BAND = 256
C = 512
NT = 2
ROWS = 16
F32 = jnp.float32
BF16 = jnp.bfloat16


class Places:
    def __init__(self):
        self.dp = lax.axis_index("dp")
        self.fr = lax.axis_index("freq")
        self.zh, self.y = self.dp // 4, self.dp % 4
        self.zl, self.x, self.c = self.fr // 8, (self.fr // 2) % 4, self.fr % 2

    def qpos(self, k):
        zl = self.zl if k < 2 else 1 - self.zl
        c = self.c if k % 2 == 0 else 1 - self.c
        return zl, c

    def q(self, k):
        zl, c = self.qpos(k)
        return (self.dp, zl * 8 + self.x * 2 + c)

    def xp(self, k):
        return (self.dp, self.zl * 8 + ((self.x + k) % 4) * 2 + self.c)

    def yp(self, k):
        return (self.zh * 4 + (self.y + k) % 4, self.fr)

    def zp(self, k):
        return (((self.zh + k) % 4) * 4 + self.y, self.fr)

    def zx(self, m):
        return (((self.zh + m) % 4) * 4 + self.y, (1 - self.zl) * 8 + self.x * 2 + self.c)

    def zo(self, k):
        zl, c = self.qpos(k)
        zh = (self.zh + jnp.where(self.zl == 1, 1, 3)) % 4
        return (zh * 4 + self.y, zl * 8 + self.x * 2 + c)

    def band(self, d):
        return (self.dp, (self.fr + 16 + d) % 16)


def sigmoid(a):
    return 1.0 / (1.0 + jnp.exp(-a))


def block_kernel(
    noisy, cot, mixing, film, embed, kern,
    out_h, gn_h, gm_h, gat_o, eg_o,
    out_o, gn_o, gm_o, npad, nlo, nhi, normed, rinv, ga, ca, mx,
    psend, pmid, precv, pown, osend, orecv, ocore, oown,
    gms, ymid, yout, yr, ys, zr, zs,
    gs, gkacc, sm, smq, smx, smr, smt, smy, smz,
    ssem, rsem, lsem, osem, order,
):
    me = Places()
    half = BAND // 2
    scale1 = film[0:1, :]
    shift = film[1:2, :]
    low_on = jnp.where(me.fr > 0, 1.0, 0.0).astype(F32)
    high_on = jnp.where(me.fr < 15, 1.0, 0.0).astype(F32)
    yrows = pl.ds(pl.multiple_of(me.y * 64, 64), 64)
    zrows = pl.ds(pl.multiple_of(me.zh * 16, 16), 16)
    mine = pl.ds(pl.multiple_of(me.y * 64 + me.zh * 16, 16), 16)
    four = pl.ds(me.zh * 4, 4)
    sent = []
    groups = {}

    def send(group, src, dst, dev):
        i = len(sent)
        copy = pltpu.make_async_remote_copy(
            src_ref=src, dst_ref=dst, send_sem=ssem.at[i], recv_sem=rsem.at[i],
            device_id=dev, device_id_type=MESH,
        )
        sent.append(copy)
        groups.setdefault(group, []).append(copy)
        copy.start()

    def arrive(*names):
        for name in names:
            for copy in groups.pop(name, []):
                copy.wait_recv()

    def all_sent():
        while sent_open := [i for i in range(len(sent)) if i not in drained]:
            for i in sent_open:
                sent[i].wait_send()
                drained.add(i)

    drained = set()
    local = {}

    def rows_loop(first, last):
        return pl.loop(first // ROWS, last // ROWS)

    def pad():
        @rows_loop(0, BAND)
        def _(r):
            base = pl.multiple_of(r * ROWS, ROWS)
            for t in range(NT):
                npad[t, pl.ds(base + 8, ROWS), :] = noisy[t, pl.ds(base, ROWS), :].astype(F32)

    barrier = pltpu.get_barrier_semaphore()
    greeted = [f(k) for f in (me.q, me.xp, me.yp, me.zp) for k in (1, 2, 3)]
    greeted += [me.band(1), me.band(-1), me.zo(3)] + [me.zx(m) for m in (1, 2, 3)]

    def greet():
        for peer in greeted:
            pl.semaphore_signal(barrier, inc=1, device_id=peer, device_id_type=MESH)

    def enter():
        pl.semaphore_wait(barrier, len(greeted))

    def halo():
        send("halo", noisy.at[:, pl.ds(0, 16), :], nhi, me.band(-1))
        send("halo", noisy.at[:, pl.ds(BAND - 16, 16), :], nlo, me.band(1))

    def ca_slot(k, t):
        return ca.at[t, pl.ds(k * BAND, BAND), :]

    def cots():
        for t in range(NT):
            send(("cotz", t), cot.at[t], ca_slot(2, t), me.q(2))
        for t in range(NT):
            send("cot", cot.at[t], ca_slot(1, t), me.q(1))

    def mix_cols(k, j):
        zl, c = me.qpos(k)
        band = zl * 8 + ((me.x + j) % 4) * 2 + c
        return mixing.at[:, pl.ds(pl.multiple_of(band * BAND, BAND), BAND)]

    def mix_slot(k, j):
        return mx.at[pl.ds(k * BAND, BAND), pl.ds(j * BAND, BAND)]

    def mix():
        for j in (2, 1, 3, 0):
            for k in (1, 2, 3):
                peer = me.q(k) if k == 1 else me.zo(k)
                send(("mix", j), mix_cols(k, j), mix_slot(k, j), peer)

    def locals_in():
        for j in range(4):
            local[j] = pltpu.make_async_copy(mix_cols(0, j), mix_slot(0, j), lsem.at[j])
        for t in range(NT):
            local[4 + t] = pltpu.make_async_copy(cot.at[t], ca_slot(0, t), lsem.at[4 + t])
        for copy in local.values():
            copy.start()

    def locals_done():
        for copy in local.values():
            copy.wait()

    def halo_rows():
        arrive("halo")
        for t in range(NT):
            npad[t, 0:8, :] = nlo[t].astype(F32)[8:16] * low_on
            npad[t, BAND + 8 : BAND + 16, :] = nhi[t].astype(F32)[0:8] * high_on

    def noisy_windows(base):
        wins = []
        for t in range(NT):
            w = npad[t, pl.ds(base, ROWS + 16), :]
            wins.append([w[7 + i : 7 + i + ROWS] for i in range(3)])
        return wins

    def gate_rows(slot, first, last):
        return ga.at[:, pl.ds(slot * BAND + first, last - first), :]

    def forward(first, last):
        @rows_loop(first, last)
        def _(r):
            base = pl.multiple_of(r * ROWS, ROWS)
            wins = noisy_windows(base)
            for t in range(NT):
                st = None
                for tp in range(NT):
                    for i in range(3):
                        term = kern[i, tp - t + 1 : tp - t + 2, :] * wins[tp][i]
                        st = term if st is None else st + term
                ri = lax.rsqrt(jnp.mean(st * st, axis=-1, keepdims=True) + 1e-05)
                nm = st * ri
                normed[t, pl.ds(base, ROWS), :] = nm
                rinv[t, pl.ds(base, ROWS), :] = jnp.broadcast_to(ri, (ROWS, 128))
                act = nm * scale1 + shift
                ga[t, pl.ds(base, ROWS), :] = (act * sigmoid(act)).astype(BF16)

    def gate_send(first, last):
        h = first // half
        send(("ga3", h), gate_rows(0, first, last), gate_rows(3, first, last), me.xp(1))
        send(("ga1", h), gate_rows(0, first, last), gate_rows(1, first, last), me.xp(3))

    def gate_right():
        arrive(("ga3", 0))
        send("ga2", gate_rows(3, 0, half), gate_rows(2, 0, half), me.xp(1))

    def gate_left():
        arrive(("ga1", 1))
        send("ga2", gate_rows(1, half, BAND), gate_rows(2, half, BAND), me.xp(3))

    def cot_pass(t):
        arrive(("cotz", t))
        send("cot", ca_slot(2, t), ca_slot(3, t), me.q(1))

    def cot_done():
        arrive("cot")
        locals_done()

    def gm_product(j):
        arrive(*{0: (), 1: (("ga1", 0), ("ga1", 1)), 2: ("ga2",), 3: (("ga3", 0), ("ga3", 1))}[j])
        acc = None
        for t in range(NT):
            part = lax.dot_general(
                ca[t], ga[t, pl.ds(j * BAND, BAND), :],
                (((1,), (1,)), ((), ())), preferred_element_type=F32,
            )
            acc = part if acc is None else acc + part
        gms[j] = acc.astype(BF16).reshape(4, BAND, BAND)

    def y_rows(m):
        return pl.ds(pl.multiple_of((me.y + m) % 4 * 64, 64), 64)

    def gm_send(j):
        near, far, back = y_rows(1), y_rows(2), y_rows(3)
        send(("ya", j), gms.at[j, pl.ds(0, 2), far, :], ymid.at[j, 0], me.yp(1))
        send(("yb", j), gms.at[j, pl.ds(2, 2), far, :], ymid.at[j, 1], me.yp(3))
        send(("y", j), gms.at[j, pl.ds(2, 2), near, :], yr.at[j, 0, pl.ds(2, 2)], me.yp(1))
        send(("y", j), gms.at[j, pl.ds(0, 2), back, :], yr.at[j, 1, pl.ds(0, 2)], me.yp(3))

    def y_join(j):
        for side, group, rows in ((0, ("ya", j), y_rows(1)), (1, ("yb", j), y_rows(3))):
            arrive(group)
            for k in range(2):
                total = gms[j, 2 * side + k, rows, :].astype(F32) + ymid[j, side, k].astype(F32)
                yout[j, side, k] = total.astype(BF16)
            send(
                ("y", j), yout.at[j, side], yr.at[j, side, pl.ds(2 * side, 2)],
                me.yp(1 if side == 0 else 3),
            )

    def y_sum(j):
        arrive(("y", j))
        for k in range(4):
            total = gms[j, k, yrows, :].astype(F32)
            for m in range(2):
                total = total + yr[j, m, k].astype(F32)
            ys[j, k] = total.astype(BF16)
        for m in (2, 1, 3, 0):
            rows = pl.ds(pl.multiple_of((me.zh + m) % 4 * 16, 16), 16)
            send(("z", j), ys.at[j, pl.ds(2, 2), rows, :], zr.at[j, 3 + m], me.zx(m))
            if m > 0:
                send(("z", j), ys.at[j, pl.ds(0, 2), rows, :], zr.at[j, m - 1], me.zp(m))

    def z_sum(j):
        arrive(("z", j))
        for far in range(2):
            for k in range(2):
                if far:
                    total = zr[j, 3, k].astype(F32)
                else:
                    total = ys[j, k, zrows, :].astype(F32)
                for m in range(3):
                    total = total + zr[j, 4 * far + m, k].astype(F32)
                if k == 0:
                    gm_o[j, mine, pl.ds(2 * far * BAND, BAND)] = total.astype(BF16)
                else:
                    zs[j, far] = total.astype(BF16)
        for far in range(2):
            cols = pl.ds((2 * far + 1) * BAND, BAND)
            send(("f", j), zs.at[j, far], gm_o.at[j, mine, cols], me.q(1))

    def z_gather(j):
        arrive(("f", j))
        for m in (2, 1, 3):
            send(("az", j), gm_o.at[j, mine], gm_o.at[j, mine], me.zp(m))

    def y_gather(j):
        arrive(("az", j))
        send(("ar", j), gm_o.at[j, yrows], gm_o.at[j, yrows], me.yp(1))
        send(("al", j), gm_o.at[j, yrows], gm_o.at[j, yrows], me.yp(3))

    def y_pass(j):
        for group, m, first, to in ((("ar", j), 3, 0, 1), (("al", j), 1, 32, 3)):
            arrive(group)
            rows = pl.ds(pl.multiple_of((me.y + m) % 4 * 64 + first, 32), 32)
            send(("ay", j), gm_o.at[j, rows], gm_o.at[j, rows], me.yp(to))

    def gate_grad(j):
        arrive(("mix", j))
        mt = mx[:, pl.ds(j * BAND, BAND)].T
        for t in range(NT):
            part = jnp.dot(mt, ca[t], preferred_element_type=F32)
            if j == 0:
                pown[t] = part
            else:
                psend[j - 1, t] = part.astype(BF16)

    def p_far():
        send("pa0", psend.at[1, 0], pmid.at[0], me.xp(1))
        send("pa1", psend.at[1, 1], pmid.at[1], me.xp(3))

    def p_right():
        send("p", psend.at[0, 1], precv.at[0, 1], me.xp(1))

    def p_left():
        send("p", psend.at[2, 0], precv.at[1, 0], me.xp(3))

    def p_join():
        arrive("pa0")
        psend[0, 0] = (psend[0, 0].astype(F32) + pmid[0].astype(F32)).astype(BF16)
        send("p", psend.at[0, 0], precv.at[0, 0], me.xp(1))
        arrive("pa1")
        psend[2, 1] = (psend[2, 1].astype(F32) + pmid[1].astype(F32)).astype(BF16)
        send("p", psend.at[2, 1], precv.at[1, 1], me.xp(3))

    def mixed(k, t):
        return jnp.dot(mx[pl.ds(k * BAND, BAND), :], ga[t], preferred_element_type=F32)

    def mixed_far():
        arrive(("ga1", 0), ("ga1", 1), "ga2", ("ga3", 0), ("ga3", 1), ("mix", 0), ("mix", 1), ("mix", 2), ("mix", 3))
        for t in range(NT):
            osend[2, t] = mixed(3, t).astype(BF16)
        send("oc", osend.at[2], ocore, me.q(1))

    def mixed_core():
        for t in range(NT):
            osend[0, t] = mixed(1, t).astype(BF16)
        send("o", osend.at[0], orecv.at[0], me.q(1))

    def mixed_z():
        parts = [mixed(2, t) for t in range(NT)]
        arrive("oc")
        for t in range(NT):
            osend[1, t] = (parts[t] + ocore[t].astype(F32)).astype(BF16)
        send("o", osend.at[1], orecv.at[1], me.q(2))

    def mixed_own():
        for t in range(NT):
            oown[t] = mixed(0, t)

    def output():
        arrive("o")

        @rows_loop(0, BAND)
        def _(r):
            rows = pl.ds(pl.multiple_of(r * ROWS, ROWS), ROWS)
            for t in range(NT):
                total = oown[t, rows, :] + noisy[t, rows, :].astype(F32)
                for m in range(2):
                    total = total + orecv[m, t, rows, :].astype(F32)
                out_o[t, rows, :] = total.astype(BF16)

    def backward():
        arrive("p")
        gkacc[...] = jnp.zeros_like(gkacc)

        @rows_loop(0, BAND)
        def _(r):
            base = pl.multiple_of(r * ROWS, ROWS)
            rows = pl.ds(base, ROWS)
            wins = noisy_windows(base)
            for t in range(NT):
                gg = pown[t, rows, :]
                for m in range(2):
                    gg = gg + precv[m, t, rows, :].astype(F32)
                nm = normed[t, rows, :]
                ri = rinv[t, rows, :][:, 0:1]
                act = nm * scale1 + shift
                sig = sigmoid(act)
                gact = gg * sig * (1.0 + act * (1.0 - sig))
                prod = gact * nm
                gkacc[9] += prod[0:8] + prod[8:16]
                gkacc[10] += gact[0:8] + gact[8:16]
                gnm = gact * scale1
                mean = jnp.mean(gnm * nm, axis=-1, keepdims=True)
                gst = ri * (gnm - nm * mean)
                gs[t, pl.ds(base + 8, ROWS), :] = gst
                for tp in range(NT):
                    for i in range(3):
                        prod = wins[tp][i] * gst
                        gkacc[i * 3 + tp - t + 1] += prod[0:8] + prod[8:16]

    def grad_halo():
        send("gs", gs.at[:, pl.ds(8, 8), :], gs.at[:, pl.ds(BAND + 8, 8), :], me.band(-1))
        send("gs", gs.at[:, pl.ds(BAND, 8), :], gs.at[:, pl.ds(0, 8), :], me.band(1))

    def sums_q():
        sm[...] = jnp.zeros_like(sm)
        for i in range(11):
            sm[i : i + 1, :] = jnp.sum(gkacc[i], axis=0, keepdims=True)
        for k in (2, 3, 1):
            send("smq", sm, smq.at[k - 1], me.q(k))

    def sums_x():
        arrive("smq")
        smt[...] = sm[...] + smq[0] + smq[1] + smq[2]
        for k in (2, 1, 3):
            send("smx", smt, smx.at[k - 1], me.xp(k))

    def sums_y():
        arrive("smx")
        smr[...] = smt[...] + smx[0] + smx[1] + smx[2]
        smy[me.y] = smr[...]
        for m in (2, 1, 3):
            send("gy", smr, smy.at[me.y], me.yp(m))

    def sums_z():
        arrive("gy")
        smz[...] = jnp.zeros_like(smz)
        smz[0:16] = smy[0] + smy[1] + smy[2] + smy[3]
        for y in range(4):
            for i in range(2):
                smz[16 + 4 * i + y : 17 + 4 * i + y, :] = smy[y, 9 + i : 10 + i, :]
        gat_o[me.zh] = smz[...]
        for m in (2, 1, 3):
            send("gz", smz, gat_o.at[me.zh], me.zp(m))

    def embeds_y():
        eg_o[me.dp] = embed[...]
        for m in (2, 1, 3):
            send("ey", embed, eg_o.at[me.dp], me.yp(m))

    def embeds_z():
        arrive("ey")
        for m in (2, 1, 3):
            send("ez", eg_o.at[four], eg_o.at[four], me.zp(m))

    def grad_back():
        arrive("gs")
        for t in range(NT):
            gs[t, 0:8, :] = gs[t, 0:8, :] * low_on
            gs[t, BAND + 8 : BAND + 16, :] = gs[t, BAND + 8 : BAND + 16, :] * high_on

        @rows_loop(0, BAND)
        def _(r):
            base = pl.multiple_of(r * ROWS, ROWS)
            rows = pl.ds(base, ROWS)
            wins = []
            for t in range(NT):
                w = gs[t, pl.ds(base, ROWS + 16), :]
                wins.append([w[9 - i : 9 - i + ROWS] for i in range(3)])
            for tp in range(NT):
                back = ca[tp, rows, :].astype(F32)
                for t in range(NT):
                    for i in range(3):
                        back = back + kern[i, tp - t + 1 : tp - t + 2, :] * wins[t][i]
                gn_o[tp, rows, :] = back.astype(BF16)

    def gm_done(j):
        arrive(("ay", j))
        local_out.append(pltpu.make_async_copy(gm_o.at[j], gm_h.at[j], osem.at[j]))
        local_out[-1].start()

    def out_done():
        local_out.append(pltpu.make_async_copy(out_o, out_h, osem.at[4]))
        local_out[-1].start()

    def back_done():
        local_out.append(pltpu.make_async_copy(gn_o, gn_h, osem.at[5]))
        local_out[-1].start()

    local_out = []
    order(types.SimpleNamespace(**locals()))
    for name in list(groups):
        arrive(name)
    all_sent()
    for copy in local_out:
        copy.wait()


N_COPIES = 2 + 6 + 12 + 10 + 6 + 3 + 4 * (6 + 7 + 2 + 3 + 4) + 2 + 12 + 6


def schedule(k):
    k.pad()
    k.greet()
    k.forward(16, 240)
    k.enter()
    k.halo()
    k.gate_send(16, 128)
    k.gate_send(128, 240)
    k.cots()
    k.mix()
    k.locals_in()
    k.embeds_y()
    k.halo_rows()
    k.forward(0, 16)
    k.forward(240, 256)
    k.gate_send(0, 16)
    k.gate_send(240, 256)
    k.cot_pass(0)
    k.embeds_z()
    k.gate_right()
    k.cot_pass(1)
    k.cot_done()
    k.gm_product(0)
    k.gm_send(0)
    k.gate_grad(2)
    k.gate_left()
    k.p_far()
    k.gm_product(3)
    k.gm_send(3)
    k.gm_product(1)
    k.gm_send(1)
    k.y_join(0)
    k.gate_grad(1)
    k.p_right()
    k.gate_grad(3)
    k.p_left()
    k.y_join(3)
    k.y_sum(0)
    k.gm_product(2)
    k.gm_send(2)
    k.y_join(1)
    k.p_join()
    k.gate_grad(0)
    k.z_sum(0)
    k.y_sum(3)
    k.y_join(2)
    k.mixed_far()
    k.y_sum(1)
    k.z_gather(0)
    k.z_sum(3)
    k.mixed_core()
    k.y_sum(2)
    k.mixed_own()
    k.y_gather(0)
    k.z_gather(3)
    k.z_sum(1)
    k.y_gather(3)
    k.z_gather(1)
    k.z_sum(2)
    k.y_pass(0)
    k.backward()
    k.grad_halo()
    k.sums_q()
    k.z_gather(2)
    k.y_gather(1)
    k.y_pass(3)
    k.mixed_z()
    k.sums_x()
    k.y_gather(2)
    k.y_pass(1)
    k.grad_back()
    k.back_done()
    k.sums_y()
    k.y_pass(2)
    k.sums_z()
    k.output()
    k.out_done()
    k.gm_done(0)
    k.gm_done(3)
    k.gm_done(1)
    k.gm_done(2)


def fused_block(noisy, cot, mixing, film, embed, kern, order=schedule, number=0):
    vmem = pl.BlockSpec(memory_space=pltpu.VMEM)
    hbm = pl.BlockSpec(memory_space=pl.ANY)
    act = (NT, BAND, C)
    full = (NT, 4 * BAND, C)
    pad = (NT, BAND + 16, C)
    return pl.pallas_call(
        functools.partial(block_kernel, order=order),
        out_shape=(
            jax.ShapeDtypeStruct(act, BF16),
            jax.ShapeDtypeStruct(act, BF16),
            jax.ShapeDtypeStruct((4, BAND, 4 * BAND), BF16),
            jax.ShapeDtypeStruct((4, 24, C), F32),
            jax.ShapeDtypeStruct((16, 1, C), F32),
        ),
        in_specs=[vmem, hbm, hbm, vmem, vmem, vmem],
        out_specs=(hbm,) * 3 + (vmem,) * 2,
        scratch_shapes=[
            pltpu.VMEM(act, BF16),
            pltpu.VMEM(act, BF16),
            pltpu.VMEM((4, BAND, 4 * BAND), BF16),
            pltpu.VMEM(pad, F32),
            pltpu.VMEM((NT, 16, C), BF16),
            pltpu.VMEM((NT, 16, C), BF16),
            pltpu.VMEM(act, F32),
            pltpu.VMEM((NT, BAND, 128), F32),
            pltpu.VMEM(full, BF16),
            pltpu.VMEM(full, BF16),
            pltpu.VMEM((4 * BAND, 4 * BAND), BF16),
            pltpu.VMEM((3,) + act, BF16),
            pltpu.VMEM(act, BF16),
            pltpu.VMEM((2,) + act, BF16),
            pltpu.VMEM(act, F32),
            pltpu.VMEM((3,) + act, BF16),
            pltpu.VMEM((2,) + act, BF16),
            pltpu.VMEM(act, BF16),
            pltpu.VMEM(act, F32),
            pltpu.VMEM((4, 4, BAND, BAND), BF16),
            pltpu.VMEM((4, 2, 2, 64, BAND), BF16),
            pltpu.VMEM((4, 2, 2, 64, BAND), BF16),
            pltpu.VMEM((4, 2, 4, 64, BAND), BF16),
            pltpu.VMEM((4, 4, 64, BAND), BF16),
            pltpu.VMEM((4, 7, 2, 16, BAND), BF16),
            pltpu.VMEM((4, 2, 16, BAND), BF16),
            pltpu.VMEM(pad, F32),
            pltpu.VMEM((11, 8, C), F32),
            pltpu.VMEM((16, C), F32),
            pltpu.VMEM((3, 16, C), F32),
            pltpu.VMEM((3, 16, C), F32),
            pltpu.VMEM((16, C), F32),
            pltpu.VMEM((16, C), F32),
            pltpu.VMEM((4, 16, C), F32),
            pltpu.VMEM((24, C), F32),
            pltpu.SemaphoreType.DMA((N_COPIES,)),
            pltpu.SemaphoreType.DMA((N_COPIES,)),
            pltpu.SemaphoreType.DMA((6,)),
            pltpu.SemaphoreType.DMA((6,)),
        ],
        compiler_params=pltpu.CompilerParams(
            collective_id=number, has_side_effects=True, vmem_limit_bytes=60 * 1024 * 1024
        ),
    )(noisy, cot, mixing, film, embed, kern)


def finish_kernel(out, gn, gm, gat, eg, out_o, gn_o, gm_o, gk_o, film_o):
    step = pl.program_id(0)
    fr = lax.axis_index("freq")
    zl, x, c = fr // 8, (fr // 2) % 4, fr % 2
    for src, dst in ((out, out_o), (gn, gn_o)):
        dst[...] = jnp.stack([src[t].astype(F32) for t in range(NT)], axis=1).astype(BF16)
    for k in range(4):
        bz = zl if k < 2 else 1 - zl
        bc = c if k % 2 == 0 else 1 - c
        for j in range(4):
            band = bz * 8 + ((x + j) % 4) * 2 + bc
            cols = pl.ds(pl.multiple_of(band * BAND, BAND), BAND)
            gm_o[:, cols] = gm[j, :, k * BAND : (k + 1) * BAND].astype(F32)
    wide = film_o.shape[0]
    embeds = eg[:, 0, pl.ds(pl.multiple_of(step * wide, wide), wide)]
    both = jnp.concatenate(
        [jnp.concatenate([gat[z, 16 + 4 * i : 20 + 4 * i] for z in range(4)]) for i in range(2)],
        axis=1,
    )
    film_o[...] = lax.dot_general(
        embeds, both, (((0,), (0,)), ((), ())),
        preferred_element_type=F32, precision=lax.Precision.HIGHEST,
    )

    @pl.when(step == 0)
    def _():
        total = jnp.sum(gat[:, 0:9, :], axis=0)
        for i in range(3):
            gk_o[i] = total[3 * i : 3 * i + 3]


def finish(out, grad_noisy, grad_mixing, sums, embeds):
    steps = 4
    rows, wide = BAND // steps, C // steps
    planes = pl.BlockSpec((NT, rows, C), lambda i: (0, i, 0))
    pairs = pl.BlockSpec((rows, NT, C), lambda i: (i, 0, 0))
    return pl.pallas_call(
        finish_kernel,
        grid=(steps,),
        out_shape=(
            jax.ShapeDtypeStruct((BAND, NT, C), BF16),
            jax.ShapeDtypeStruct((BAND, NT, C), BF16),
            jax.ShapeDtypeStruct((BAND, 16 * BAND), F32),
            jax.ShapeDtypeStruct((3, 3, C), F32),
            jax.ShapeDtypeStruct((C, 2 * C), F32),
        ),
        in_specs=[
            planes,
            planes,
            pl.BlockSpec((4, rows, 4 * BAND), lambda i: (0, i, 0)),
            pl.BlockSpec((4, 24, C), lambda i: (0, 0, 0)),
            pl.BlockSpec((16, 1, C), lambda i: (0, 0, 0)),
        ],
        out_specs=(
            pairs,
            pairs,
            pl.BlockSpec((rows, 16 * BAND), lambda i: (i, 0)),
            pl.BlockSpec((3, 3, C), lambda i: (0, 0, 0)),
            pl.BlockSpec((wide, 2 * C), lambda i: (i, 0)),
        ),
        compiler_params=pltpu.CompilerParams(vmem_limit_bytes=60 * 1024 * 1024),
    )(out, grad_noisy, grad_mixing, sums, embeds)


def embed_steps(timestep, width):
    half = width // 2
    freqs = jnp.exp(-math.log(10000.0) * jnp.arange(half, dtype=jnp.float32) / half)
    angles = timestep.astype(jnp.float32)[:, None] * freqs[None, :]
    return jnp.concatenate([jnp.sin(angles), jnp.cos(angles)], axis=1).astype(jnp.bfloat16)


def on_device(noisy, timestep, kernel, film_weight, mixing, cotangent):
    embed = embed_steps(timestep, C)
    film = jnp.dot(embed, film_weight, preferred_element_type=jnp.float32)
    film = jnp.concatenate([1.0 + film[:, :C], film[:, C:]], axis=0)
    planes = [jnp.transpose(a[0], (1, 0, 2)) for a in (noisy, cotangent)]
    out, grad_noisy, grad_mixing, sums, embeds = fused_block(
        planes[0], planes[1], mixing, film, embed.astype(F32), kernel
    )
    output, grad_noisy, grad_mixing, grad_kernel, grad_film = finish(
        out, grad_noisy, grad_mixing, sums, embeds
    )
    output, grad_noisy = output[None], grad_noisy[None]
    return (output, grad_noisy, grad_mixing, grad_kernel, grad_film)


def solution(mesh):
    return jax.shard_map(
        on_device,
        mesh=mesh,
        in_specs=(
            P("dp", "freq", None, None),
            P("dp"),
            P(),
            P(),
            P("freq", None),
            P("dp", "freq", None, None),
        ),
        out_specs=(
            P("dp", "freq", None, None),
            P("dp", "freq", None, None),
            P("freq", None),
            P(),
            P(),
        ),
        check_vma=False,
    )
```

```python
import functools
import math
import types

import jax
import jax.numpy as jnp
from jax import lax
from jax.experimental import pallas as pl
from jax.experimental.pallas import tpu as pltpu
from jax.sharding import PartitionSpec as P

MESH = pl.DeviceIdType.MESH
BAND = 256
C = 512
NT = 2
ROWS = 16
F32 = jnp.float32
BF16 = jnp.bfloat16


class Places:
    def __init__(self):
        self.dp = lax.axis_index("dp")
        self.fr = lax.axis_index("freq")
        self.zh, self.y = self.dp // 4, self.dp % 4
        self.zl, self.x, self.c = self.fr // 8, (self.fr // 2) % 4, self.fr % 2

    def qpos(self, k):
        zl = self.zl if k < 2 else 1 - self.zl
        c = self.c if k % 2 == 0 else 1 - self.c
        return zl, c

    def q(self, k):
        zl, c = self.qpos(k)
        return (self.dp, zl * 8 + self.x * 2 + c)

    def xp(self, k):
        return (self.dp, self.zl * 8 + ((self.x + k) % 4) * 2 + self.c)

    def yp(self, k):
        return (self.zh * 4 + (self.y + k) % 4, self.fr)

    def zp(self, k):
        return (((self.zh + k) % 4) * 4 + self.y, self.fr)

    def zx(self, m):
        return (((self.zh + m) % 4) * 4 + self.y, (1 - self.zl) * 8 + self.x * 2 + self.c)

    def zo(self, k):
        zl, c = self.qpos(k)
        zh = (self.zh + jnp.where(self.zl == 1, 1, 3)) % 4
        return (zh * 4 + self.y, zl * 8 + self.x * 2 + c)

    def band(self, d):
        return (self.dp, (self.fr + 16 + d) % 16)


def sigmoid(a):
    return 1.0 / (1.0 + jnp.exp(-a))


def block_kernel(
    noisy, cot, mixing, film, embed, kern,
    out_h, gn_h, gm_h, gat_o, eg_o,
    out_o, gn_o, gm_o, npad, normed, rinv, ga, ca, mx,
    psend, pmid, precv, pown, osend, orecv, ocore, oown,
    gms, ymid, yout, yr, ys, zr, zs,
    gs, gkacc, sm, smq, smx, smr, smt, smy, smz,
    ssem, rsem, lsem, osem, order,
):
    me = Places()
    half = BAND // 2
    scale1 = film[0:1, :]
    shift = film[1:2, :]
    low_on = jnp.where(me.fr > 0, 1.0, 0.0).astype(F32)
    high_on = jnp.where(me.fr < 15, 1.0, 0.0).astype(F32)
    yrows = pl.ds(pl.multiple_of(me.y * 64, 64), 64)
    zrows = pl.ds(pl.multiple_of(me.zh * 16, 16), 16)
    mine = pl.ds(pl.multiple_of(me.y * 64 + me.zh * 16, 16), 16)
    four = pl.ds(me.zh * 4, 4)
    sent = []
    groups = {}

    def send(group, src, dst, dev):
        i = len(sent)
        copy = pltpu.make_async_remote_copy(
            src_ref=src, dst_ref=dst, send_sem=ssem.at[i], recv_sem=rsem.at[i],
            device_id=dev, device_id_type=MESH,
        )
        sent.append(copy)
        groups.setdefault(group, []).append(copy)
        copy.start()

    def arrive(*names):
        for name in names:
            for copy in groups.pop(name, []):
                copy.wait_recv()

    def all_sent():
        while sent_open := [i for i in range(len(sent)) if i not in drained]:
            for i in sent_open:
                sent[i].wait_send()
                drained.add(i)

    drained = set()
    local = {}

    def rows_loop(first, last):
        return pl.loop(first // ROWS, last // ROWS)

    def pad():
        @rows_loop(0, BAND)
        def _(r):
            base = pl.multiple_of(r * ROWS, ROWS)
            for t in range(NT):
                npad[t, pl.ds(base + 8, ROWS), :] = noisy[pl.ds(base, ROWS), t, :].astype(F32)

    def own_cot():
        @rows_loop(0, BAND)
        def _(r):
            rows = pl.ds(pl.multiple_of(r * ROWS, ROWS), ROWS)
            for t in range(NT):
                ca[t, rows, :] = cot[rows, t, :]

    barrier = pltpu.get_barrier_semaphore()
    greeted = [f(k) for f in (me.q, me.xp, me.yp, me.zp) for k in (1, 2, 3)]
    greeted += [me.band(1), me.band(-1), me.zo(3)] + [me.zx(m) for m in (1, 2, 3)]

    def greet():
        for peer in greeted:
            pl.semaphore_signal(barrier, inc=1, device_id=peer, device_id_type=MESH)

    def enter():
        pl.semaphore_wait(barrier, len(greeted))

    def halo():
        send("halo", npad.at[:, pl.ds(8, 8), :], npad.at[:, pl.ds(BAND + 8, 8), :], me.band(-1))
        send("halo", npad.at[:, pl.ds(BAND, 8), :], npad.at[:, pl.ds(0, 8), :], me.band(1))

    def ca_slot(k, t):
        return ca.at[t, pl.ds(k * BAND, BAND), :]

    def cots():
        for t in range(NT):
            send(("cotz", t), ca_slot(0, t), ca_slot(2, t), me.q(2))
        for t in range(NT):
            send("cot", ca_slot(0, t), ca_slot(1, t), me.q(1))

    def mix_cols(k, j):
        zl, c = me.qpos(k)
        band = zl * 8 + ((me.x + j) % 4) * 2 + c
        return mixing.at[:, pl.ds(pl.multiple_of(band * BAND, BAND), BAND)]

    def mix_slot(k, j):
        return mx.at[pl.ds(k * BAND, BAND), pl.ds(j * BAND, BAND)]

    def mix():
        for j in (2, 1, 3, 0):
            for k in (1, 2, 3):
                peer = me.q(k) if k == 1 else me.zo(k)
                send(("mix", j), mix_cols(k, j), mix_slot(k, j), peer)

    def locals_in():
        for j in range(4):
            local[j] = pltpu.make_async_copy(mix_cols(0, j), mix_slot(0, j), lsem.at[j])
        for copy in local.values():
            copy.start()

    def locals_done():
        for copy in local.values():
            copy.wait()

    def halo_rows():
        arrive("halo")
        for t in range(NT):
            npad[t, 0:8, :] = npad[t, 0:8, :] * low_on
            npad[t, BAND + 8 : BAND + 16, :] = npad[t, BAND + 8 : BAND + 16, :] * high_on

    def noisy_windows(base):
        wins = []
        for t in range(NT):
            w = npad[t, pl.ds(base, ROWS + 16), :]
            wins.append([w[7 + i : 7 + i + ROWS] for i in range(3)])
        return wins

    def gate_rows(slot, first, last):
        return ga.at[:, pl.ds(slot * BAND + first, last - first), :]

    def forward(first, last):
        @rows_loop(first, last)
        def _(r):
            base = pl.multiple_of(r * ROWS, ROWS)
            wins = noisy_windows(base)
            for t in range(NT):
                st = None
                for tp in range(NT):
                    for i in range(3):
                        term = kern[i, tp - t + 1 : tp - t + 2, :] * wins[tp][i]
                        st = term if st is None else st + term
                ri = lax.rsqrt(jnp.mean(st * st, axis=-1, keepdims=True) + 1e-05)
                nm = st * ri
                normed[t, pl.ds(base, ROWS), :] = nm
                rinv[t, pl.ds(base, ROWS), :] = jnp.broadcast_to(ri, (ROWS, 128))
                act = nm * scale1 + shift
                ga[t, pl.ds(base, ROWS), :] = (act * sigmoid(act)).astype(BF16)

    def gate_send(first, last):
        h = first // half + (0 if last - first > ROWS else 2)
        send(("ga3", h), gate_rows(0, first, last), gate_rows(3, first, last), me.xp(1))
        send(("ga1", h), gate_rows(0, first, last), gate_rows(1, first, last), me.xp(3))

    def gate_right(first, last):
        arrive(("ga3", 0 if last - first > ROWS else 2))
        send("ga2", gate_rows(3, first, last), gate_rows(2, first, last), me.xp(1))

    def gate_left(first, last):
        arrive(("ga1", 1 if last - first > ROWS else 3))
        send("ga2", gate_rows(1, first, last), gate_rows(2, first, last), me.xp(3))

    def gate_all(*slots):
        for slot in slots:
            if slot == 2:
                arrive("ga2")
            else:
                arrive(*[("ga3" if slot == 3 else "ga1", h) for h in range(4)])

    def cot_pass(t):
        arrive(("cotz", t))
        send("cot", ca_slot(2, t), ca_slot(3, t), me.q(1))

    def cot_done():
        arrive("cot")
        locals_done()

    def gm_product(j):
        if j > 0:
            gate_all(j)
        acc = None
        for t in range(NT):
            part = lax.dot_general(
                ca[t], ga[t, pl.ds(j * BAND, BAND), :],
                (((1,), (1,)), ((), ())), preferred_element_type=F32,
            )
            acc = part if acc is None else acc + part
        gms[j] = acc.astype(BF16).reshape(4, BAND, BAND)

    def y_rows(m):
        return pl.ds(pl.multiple_of((me.y + m) % 4 * 64, 64), 64)

    def gm_send(j):
        near, far, back = y_rows(1), y_rows(2), y_rows(3)
        send(("ya", j), gms.at[j, pl.ds(0, 2), far, :], ymid.at[j, 0], me.yp(1))
        send(("yb", j), gms.at[j, pl.ds(2, 2), far, :], ymid.at[j, 1], me.yp(3))
        send(("y", j), gms.at[j, pl.ds(2, 2), near, :], yr.at[j, 0, pl.ds(2, 2)], me.yp(1))
        send(("y", j), gms.at[j, pl.ds(0, 2), back, :], yr.at[j, 1, pl.ds(0, 2)], me.yp(3))

    def y_join(j):
        for side, group, rows in ((0, ("ya", j), y_rows(1)), (1, ("yb", j), y_rows(3))):
            arrive(group)
            for k in range(2):
                total = gms[j, 2 * side + k, rows, :].astype(F32) + ymid[j, side, k].astype(F32)
                yout[j, side, k] = total.astype(BF16)
            send(
                ("y", j), yout.at[j, side], yr.at[j, side, pl.ds(2 * side, 2)],
                me.yp(1 if side == 0 else 3),
            )

    def y_sum(j):
        arrive(("y", j))
        for k in range(4):
            total = gms[j, k, yrows, :].astype(F32)
            for m in range(2):
                total = total + yr[j, m, k].astype(F32)
            ys[j, k] = total.astype(BF16)
        for m in (2, 1, 3, 0):
            rows = pl.ds(pl.multiple_of((me.zh + m) % 4 * 16, 16), 16)
            send(("z", j), ys.at[j, pl.ds(2, 2), rows, :], zr.at[j, 3 + m], me.zx(m))
            if m > 0:
                send(("z", j), ys.at[j, pl.ds(0, 2), rows, :], zr.at[j, m - 1], me.zp(m))

    def z_sum(j):
        arrive(("z", j))
        for far in range(2):
            for k in range(2):
                if far:
                    total = zr[j, 3, k].astype(F32)
                else:
                    total = ys[j, k, zrows, :].astype(F32)
                for m in range(3):
                    total = total + zr[j, 4 * far + m, k].astype(F32)
                if k == 0:
                    gm_o[j, mine, pl.ds(2 * far * BAND, BAND)] = total.astype(BF16)
                else:
                    zs[j, far] = total.astype(BF16)
        for far in range(2):
            cols = pl.ds((2 * far + 1) * BAND, BAND)
            send(("f", j), zs.at[j, far], gm_o.at[j, mine, cols], me.q(1))

    def z_gather(j):
        arrive(("f", j))
        for m in (2, 1, 3):
            send(("az", j), gm_o.at[j, mine], gm_o.at[j, mine], me.zp(m))

    def y_gather(j):
        arrive(("az", j))
        send(("ar", j), gm_o.at[j, yrows], gm_o.at[j, yrows], me.yp(1))
        send(("al", j), gm_o.at[j, yrows], gm_o.at[j, yrows], me.yp(3))

    def y_pass(j):
        for group, m, first, to in ((("ar", j), 3, 0, 1), (("al", j), 1, 32, 3)):
            arrive(group)
            rows = pl.ds(pl.multiple_of((me.y + m) % 4 * 64 + first, 32), 32)
            send(("ay", j), gm_o.at[j, rows], gm_o.at[j, rows], me.yp(to))

    def gate_grad(j):
        arrive(("mix", j))
        mt = mx[:, pl.ds(j * BAND, BAND)].T
        for t in range(NT):
            part = jnp.dot(mt, ca[t], preferred_element_type=F32)
            if j == 0:
                pown[t] = part
            else:
                psend[j - 1, t] = part.astype(BF16)

    def p_far():
        send("pa0", psend.at[1, 0], pmid.at[0], me.xp(1))
        send("pa1", psend.at[1, 1], pmid.at[1], me.xp(3))

    def p_right():
        send("p", psend.at[0, 1], precv.at[0, 1], me.xp(1))

    def p_left():
        send("p", psend.at[2, 0], precv.at[1, 0], me.xp(3))

    def p_join():
        arrive("pa0")
        psend[0, 0] = (psend[0, 0].astype(F32) + pmid[0].astype(F32)).astype(BF16)
        send("p", psend.at[0, 0], precv.at[0, 0], me.xp(1))
        arrive("pa1")
        psend[2, 1] = (psend[2, 1].astype(F32) + pmid[1].astype(F32)).astype(BF16)
        send("p", psend.at[2, 1], precv.at[1, 1], me.xp(3))

    def mixed(k, t):
        return jnp.dot(mx[pl.ds(k * BAND, BAND), :], ga[t], preferred_element_type=F32)

    def mixed_far():
        gate_all(1, 2, 3)
        arrive(*[("mix", j) for j in range(4)])
        for t in range(NT):
            osend[2, t] = mixed(3, t).astype(BF16)
        send("oc", osend.at[2], ocore, me.q(1))

    def mixed_core():
        for t in range(NT):
            osend[0, t] = mixed(1, t).astype(BF16)
        send("o", osend.at[0], orecv.at[0], me.q(1))

    def mixed_z():
        parts = [mixed(2, t) for t in range(NT)]
        arrive("oc")
        for t in range(NT):
            osend[1, t] = (parts[t] + ocore[t].astype(F32)).astype(BF16)
        send("o", osend.at[1], orecv.at[1], me.q(2))

    def mixed_own():
        for t in range(NT):
            oown[t] = mixed(0, t)

    def output():
        arrive("o")

        @rows_loop(0, BAND)
        def _(r):
            base = pl.multiple_of(r * ROWS, ROWS)
            rows = pl.ds(base, ROWS)
            for t in range(NT):
                total = oown[t, rows, :] + npad[t, pl.ds(base + 8, ROWS), :]
                for m in range(2):
                    total = total + orecv[m, t, rows, :].astype(F32)
                out_o[t, rows, :] = total.astype(BF16)

    def backward():
        arrive("p")
        gkacc[...] = jnp.zeros_like(gkacc)

        @rows_loop(0, BAND)
        def _(r):
            base = pl.multiple_of(r * ROWS, ROWS)
            rows = pl.ds(base, ROWS)
            wins = noisy_windows(base)
            for t in range(NT):
                gg = pown[t, rows, :]
                for m in range(2):
                    gg = gg + precv[m, t, rows, :].astype(F32)
                nm = normed[t, rows, :]
                ri = rinv[t, rows, :][:, 0:1]
                act = nm * scale1 + shift
                sig = sigmoid(act)
                gact = gg * sig * (1.0 + act * (1.0 - sig))
                prod = gact * nm
                gkacc[9] += prod[0:8] + prod[8:16]
                gkacc[10] += gact[0:8] + gact[8:16]
                gnm = gact * scale1
                mean = jnp.mean(gnm * nm, axis=-1, keepdims=True)
                gst = ri * (gnm - nm * mean)
                gs[t, pl.ds(base + 8, ROWS), :] = gst
                for tp in range(NT):
                    for i in range(3):
                        prod = wins[tp][i] * gst
                        gkacc[i * 3 + tp - t + 1] += prod[0:8] + prod[8:16]

    def grad_halo():
        send("gs", gs.at[:, pl.ds(8, 8), :], gs.at[:, pl.ds(BAND + 8, 8), :], me.band(-1))
        send("gs", gs.at[:, pl.ds(BAND, 8), :], gs.at[:, pl.ds(0, 8), :], me.band(1))

    def sums_q():
        sm[...] = jnp.zeros_like(sm)
        for i in range(11):
            sm[i : i + 1, :] = jnp.sum(gkacc[i], axis=0, keepdims=True)
        for k in (2, 3, 1):
            send("smq", sm, smq.at[k - 1], me.q(k))

    def sums_x():
        arrive("smq")
        smt[...] = sm[...] + smq[0] + smq[1] + smq[2]
        for k in (2, 1, 3):
            send("smx", smt, smx.at[k - 1], me.xp(k))

    def sums_y():
        arrive("smx")
        smr[...] = smt[...] + smx[0] + smx[1] + smx[2]
        smy[me.y] = smr[...]
        for m in (2, 1, 3):
            send("gy", smr, smy.at[me.y], me.yp(m))

    def sums_z():
        arrive("gy")
        smz[...] = jnp.zeros_like(smz)
        smz[0:16] = smy[0] + smy[1] + smy[2] + smy[3]
        for y in range(4):
            for i in range(2):
                smz[16 + 4 * i + y : 17 + 4 * i + y, :] = smy[y, 9 + i : 10 + i, :]
        gat_o[me.zh] = smz[...]
        for m in (2, 1, 3):
            send("gz", smz, gat_o.at[me.zh], me.zp(m))

    def embeds_y():
        eg_o[me.dp] = embed[...]
        for m in (2, 1, 3):
            send("ey", embed, eg_o.at[me.dp], me.yp(m))

    def embeds_z():
        arrive("ey")
        for m in (2, 1, 3):
            send("ez", eg_o.at[four], eg_o.at[four], me.zp(m))

    def grad_back():
        arrive("gs")
        for t in range(NT):
            gs[t, 0:8, :] = gs[t, 0:8, :] * low_on
            gs[t, BAND + 8 : BAND + 16, :] = gs[t, BAND + 8 : BAND + 16, :] * high_on

        @rows_loop(0, BAND)
        def _(r):
            base = pl.multiple_of(r * ROWS, ROWS)
            rows = pl.ds(base, ROWS)
            wins = []
            for t in range(NT):
                w = gs[t, pl.ds(base, ROWS + 16), :]
                wins.append([w[9 - i : 9 - i + ROWS] for i in range(3)])
            for tp in range(NT):
                back = ca[tp, rows, :].astype(F32)
                for t in range(NT):
                    for i in range(3):
                        back = back + kern[i, tp - t + 1 : tp - t + 2, :] * wins[t][i]
                gn_o[tp, rows, :] = back.astype(BF16)

    def gm_done(j):
        arrive(("ay", j))
        local_out.append(pltpu.make_async_copy(gm_o.at[j], gm_h.at[j], osem.at[j]))
        local_out[-1].start()

    def out_done():
        local_out.append(pltpu.make_async_copy(out_o, out_h, osem.at[4]))
        local_out[-1].start()

    def back_done():
        local_out.append(pltpu.make_async_copy(gn_o, gn_h, osem.at[5]))
        local_out[-1].start()

    local_out = []
    order(types.SimpleNamespace(**locals()))
    for name in list(groups):
        arrive(name)
    all_sent()
    for copy in local_out:
        copy.wait()


N_COPIES = 2 + 6 + 12 + 12 + 6 + 3 + 4 * (6 + 7 + 2 + 3 + 4) + 2 + 12 + 6


def schedule(k):
    k.greet()
    k.pad()
    k.own_cot()
    k.forward(16, 240)
    k.enter()
    k.halo()
    k.gate_send(16, 128)
    k.gate_send(128, 240)
    k.cots()
    k.halo_rows()
    k.forward(0, 16)
    k.forward(240, 256)
    k.gate_send(0, 16)
    k.gate_send(240, 256)
    k.mix()
    k.locals_in()
    k.embeds_y()
    k.gate_right(16, 128)
    k.cot_pass(0)
    k.embeds_z()
    k.gate_left(128, 240)
    k.cot_pass(1)
    k.gate_right(0, 16)
    k.gate_left(240, 256)
    k.cot_done()
    k.gm_product(0)
    k.gm_send(0)
    k.gm_product(3)
    k.gm_send(3)
    k.gm_product(1)
    k.gm_send(1)
    k.gate_grad(2)
    k.p_far()
    k.y_join(0)
    k.gate_grad(1)
    k.p_right()
    k.gate_grad(3)
    k.p_left()
    k.y_join(3)
    k.y_sum(0)
    k.gm_product(2)
    k.gm_send(2)
    k.y_join(1)
    k.p_join()
    k.gate_grad(0)
    k.z_sum(0)
    k.y_sum(3)
    k.y_join(2)
    k.mixed_far()
    k.y_sum(1)
    k.z_gather(0)
    k.z_sum(3)
    k.mixed_core()
    k.y_sum(2)
    k.mixed_own()
    k.y_gather(0)
    k.z_gather(3)
    k.z_sum(1)
    k.y_gather(3)
    k.z_gather(1)
    k.z_sum(2)
    k.y_pass(0)
    k.backward()
    k.grad_halo()
    k.sums_q()
    k.z_gather(2)
    k.y_gather(1)
    k.y_pass(3)
    k.mixed_z()
    k.sums_x()
    k.y_gather(2)
    k.y_pass(1)
    k.grad_back()
    k.back_done()
    k.sums_y()
    k.y_pass(2)
    k.sums_z()
    k.output()
    k.out_done()
    k.gm_done(0)
    k.gm_done(3)
    k.gm_done(1)
    k.gm_done(2)


def fused_block(noisy, cot, mixing, film, embed, kern, order=schedule, number=0):
    vmem = pl.BlockSpec(memory_space=pltpu.VMEM)
    hbm = pl.BlockSpec(memory_space=pl.ANY)
    act = (NT, BAND, C)
    full = (NT, 4 * BAND, C)
    pad = (NT, BAND + 16, C)
    return pl.pallas_call(
        functools.partial(block_kernel, order=order),
        out_shape=(
            jax.ShapeDtypeStruct(act, BF16),
            jax.ShapeDtypeStruct(act, BF16),
            jax.ShapeDtypeStruct((4, BAND, 4 * BAND), BF16),
            jax.ShapeDtypeStruct((4, 24, C), F32),
            jax.ShapeDtypeStruct((16, 1, C), F32),
        ),
        in_specs=[vmem, vmem, hbm, vmem, vmem, vmem],
        out_specs=(hbm,) * 3 + (vmem,) * 2,
        scratch_shapes=[
            pltpu.VMEM(act, BF16),
            pltpu.VMEM(act, BF16),
            pltpu.VMEM((4, BAND, 4 * BAND), BF16),
            pltpu.VMEM(pad, F32),
            pltpu.VMEM(act, F32),
            pltpu.VMEM((NT, BAND, 128), F32),
            pltpu.VMEM(full, BF16),
            pltpu.VMEM(full, BF16),
            pltpu.VMEM((4 * BAND, 4 * BAND), BF16),
            pltpu.VMEM((3,) + act, BF16),
            pltpu.VMEM(act, BF16),
            pltpu.VMEM((2,) + act, BF16),
            pltpu.VMEM(act, F32),
            pltpu.VMEM((3,) + act, BF16),
            pltpu.VMEM((2,) + act, BF16),
            pltpu.VMEM(act, BF16),
            pltpu.VMEM(act, F32),
            pltpu.VMEM((4, 4, BAND, BAND), BF16),
            pltpu.VMEM((4, 2, 2, 64, BAND), BF16),
            pltpu.VMEM((4, 2, 2, 64, BAND), BF16),
            pltpu.VMEM((4, 2, 4, 64, BAND), BF16),
            pltpu.VMEM((4, 4, 64, BAND), BF16),
            pltpu.VMEM((4, 7, 2, 16, BAND), BF16),
            pltpu.VMEM((4, 2, 16, BAND), BF16),
            pltpu.VMEM(pad, F32),
            pltpu.VMEM((11, 8, C), F32),
            pltpu.VMEM((16, C), F32),
            pltpu.VMEM((3, 16, C), F32),
            pltpu.VMEM((3, 16, C), F32),
            pltpu.VMEM((16, C), F32),
            pltpu.VMEM((16, C), F32),
            pltpu.VMEM((4, 16, C), F32),
            pltpu.VMEM((24, C), F32),
            pltpu.SemaphoreType.DMA((N_COPIES,)),
            pltpu.SemaphoreType.DMA((N_COPIES,)),
            pltpu.SemaphoreType.DMA((4,)),
            pltpu.SemaphoreType.DMA((6,)),
        ],
        compiler_params=pltpu.CompilerParams(
            collective_id=number, has_side_effects=True, vmem_limit_bytes=60 * 1024 * 1024
        ),
    )(noisy, cot, mixing, film, embed, kern)


def finish_kernel(out, gn, gm, gat, eg, out_o, gn_o, gm_o, gk_o, film_o):
    step = pl.program_id(0)
    fr = lax.axis_index("freq")
    zl, x, c = fr // 8, (fr // 2) % 4, fr % 2
    for src, dst in ((out, out_o), (gn, gn_o)):
        rows = src.shape[1]
        row = lax.broadcasted_iota(jnp.int32, (2 * rows, rows), 0)
        col = lax.broadcasted_iota(jnp.int32, (2 * rows, rows), 1)
        pairs = None
        for t in range(NT):
            pick = (row == 2 * col + t).astype(F32).astype(BF16)
            part = jnp.dot(pick, src[t], preferred_element_type=F32)
            pairs = part if pairs is None else pairs + part
        dst[...] = pairs.astype(BF16).reshape(rows, NT, C)
    for k in range(4):
        bz = zl if k < 2 else 1 - zl
        bc = c if k % 2 == 0 else 1 - c
        for j in range(4):
            band = bz * 8 + ((x + j) % 4) * 2 + bc
            cols = pl.ds(pl.multiple_of(band * BAND, BAND), BAND)
            gm_o[:, cols] = gm[j, :, k * BAND : (k + 1) * BAND].astype(F32)
    wide = film_o.shape[0]
    embeds = eg[:, 0, pl.ds(pl.multiple_of(step * wide, wide), wide)]
    both = jnp.concatenate(
        [jnp.concatenate([gat[z, 16 + 4 * i : 20 + 4 * i] for z in range(4)]) for i in range(2)],
        axis=1,
    )
    parts = []
    for _ in range(3):
        parts.append(both.astype(BF16))
        both = both - parts[-1].astype(F32)
    film_o[...] = lax.dot_general(
        jnp.concatenate([embeds.astype(BF16)] * 3), jnp.concatenate(parts),
        (((0,), (0,)), ((), ())), preferred_element_type=F32,
    )

    @pl.when(step == 0)
    def _():
        total = jnp.sum(gat[:, 0:9, :], axis=0)
        for i in range(3):
            gk_o[i] = total[3 * i : 3 * i + 3]


def finish(out, grad_noisy, grad_mixing, sums, embeds):
    steps = 4
    rows, wide = BAND // steps, C // steps
    planes = pl.BlockSpec((NT, rows, C), lambda i: (0, i, 0))
    pairs = pl.BlockSpec((rows, NT, C), lambda i: (i, 0, 0))
    return pl.pallas_call(
        finish_kernel,
        grid=(steps,),
        out_shape=(
            jax.ShapeDtypeStruct((BAND, NT, C), BF16),
            jax.ShapeDtypeStruct((BAND, NT, C), BF16),
            jax.ShapeDtypeStruct((BAND, 16 * BAND), F32),
            jax.ShapeDtypeStruct((3, 3, C), F32),
            jax.ShapeDtypeStruct((C, 2 * C), F32),
        ),
        in_specs=[
            planes,
            planes,
            pl.BlockSpec((4, rows, 4 * BAND), lambda i: (0, i, 0)),
            pl.BlockSpec((4, 24, C), lambda i: (0, 0, 0)),
            pl.BlockSpec((16, 1, C), lambda i: (0, 0, 0)),
        ],
        out_specs=(
            pairs,
            pairs,
            pl.BlockSpec((rows, 16 * BAND), lambda i: (i, 0)),
            pl.BlockSpec((3, 3, C), lambda i: (0, 0, 0)),
            pl.BlockSpec((wide, 2 * C), lambda i: (i, 0)),
        ),
        compiler_params=pltpu.CompilerParams(vmem_limit_bytes=60 * 1024 * 1024),
    )(out, grad_noisy, grad_mixing, sums, embeds)


def embed_steps(timestep, width):
    half = width // 2
    freqs = jnp.exp(-math.log(10000.0) * jnp.arange(half, dtype=jnp.float32) / half)
    angles = timestep.astype(jnp.float32)[:, None] * freqs[None, :]
    return jnp.concatenate([jnp.sin(angles), jnp.cos(angles)], axis=1).astype(jnp.bfloat16)


def on_device(noisy, timestep, kernel, film_weight, mixing, cotangent):
    embed = embed_steps(timestep, C)
    film = jnp.dot(embed, film_weight, preferred_element_type=jnp.float32)
    film = jnp.concatenate([1.0 + film[:, :C], film[:, C:]], axis=0)
    out, grad_noisy, grad_mixing, sums, embeds = fused_block(
        noisy[0], cotangent[0], mixing, film, embed.astype(F32), kernel
    )
    output, grad_noisy, grad_mixing, grad_kernel, grad_film = finish(
        out, grad_noisy, grad_mixing, sums, embeds
    )
    output, grad_noisy = output[None], grad_noisy[None]
    return (output, grad_noisy, grad_mixing, grad_kernel, grad_film)


def solution(mesh):
    return jax.shard_map(
        on_device,
        mesh=mesh,
        in_specs=(
            P("dp", "freq", None, None),
            P("dp"),
            P(),
            P(),
            P("freq", None),
            P("dp", "freq", None, None),
        ),
        out_specs=(
            P("dp", "freq", None, None),
            P("dp", "freq", None, None),
            P("freq", None),
            P(),
            P(),
        ),
        check_vma=False,
    )
```

```python
import functools
import math
import types

import jax
import jax.numpy as jnp
from jax import lax
from jax.experimental import pallas as pl
from jax.experimental.pallas import tpu as pltpu
from jax.sharding import PartitionSpec as P

MESH = pl.DeviceIdType.MESH
BAND = 256
C = 512
NT = 2
ROWS = 16
F32 = jnp.float32
BF16 = jnp.bfloat16


class Places:
    def __init__(self):
        self.dp = lax.axis_index("dp")
        self.fr = lax.axis_index("freq")
        self.zh, self.y = self.dp // 4, self.dp % 4
        self.zl, self.x, self.c = self.fr // 8, (self.fr // 2) % 4, self.fr % 2

    def qpos(self, k):
        zl = self.zl if k < 2 else 1 - self.zl
        c = self.c if k % 2 == 0 else 1 - self.c
        return zl, c

    def q(self, k):
        zl, c = self.qpos(k)
        return (self.dp, zl * 8 + self.x * 2 + c)

    def xp(self, k):
        return (self.dp, self.zl * 8 + ((self.x + k) % 4) * 2 + self.c)

    def yp(self, k):
        return (self.zh * 4 + (self.y + k) % 4, self.fr)

    def zp(self, k):
        return (((self.zh + k) % 4) * 4 + self.y, self.fr)

    def zx(self, m):
        return (((self.zh + m) % 4) * 4 + self.y, (1 - self.zl) * 8 + self.x * 2 + self.c)

    def zo(self, k):
        zl, c = self.qpos(k)
        zh = (self.zh + jnp.where(self.zl == 1, 1, 3)) % 4
        return (zh * 4 + self.y, zl * 8 + self.x * 2 + c)

    def band(self, d):
        return (self.dp, (self.fr + 16 + d) % 16)


def sigmoid(a):
    return 1.0 / (1.0 + jnp.exp(-a))


def block_kernel(
    noisy, cot, mixing, film, embed, kern,
    out_h, gn_h, gm_h, gat_o, eg_o,
    out_o, gn_o, gm_o, npad, normed, rinv, ga, ca, mx,
    psend, pmid, precv, pown, osend, orecv, ocore, oown,
    gms, ymid, yout, yr, ys, zr, zs,
    gs, gkacc, sm, smq, smx, smr, smt, smy, smz,
    ssem, rsem, lsem, osem, order,
):
    me = Places()
    half = BAND // 2
    scale1 = film[0:1, :]
    shift = film[1:2, :]
    low_on = jnp.where(me.fr > 0, 1.0, 0.0).astype(F32)
    high_on = jnp.where(me.fr < 15, 1.0, 0.0).astype(F32)
    yrows = pl.ds(pl.multiple_of(me.y * 64, 64), 64)
    zrows = pl.ds(pl.multiple_of(me.zh * 16, 16), 16)
    mine = pl.ds(pl.multiple_of(me.y * 64 + me.zh * 16, 16), 16)
    four = pl.ds(me.zh * 4, 4)
    sent = []
    groups = {}

    def send(group, src, dst, dev):
        i = len(sent)
        copy = pltpu.make_async_remote_copy(
            src_ref=src, dst_ref=dst, send_sem=ssem.at[i], recv_sem=rsem.at[i],
            device_id=dev, device_id_type=MESH,
        )
        sent.append(copy)
        groups.setdefault(group, []).append(copy)
        copy.start()

    def arrive(*names):
        for name in names:
            for copy in groups.pop(name, []):
                copy.wait_recv()

    def all_sent():
        while sent_open := [i for i in range(len(sent)) if i not in drained]:
            for i in sent_open:
                sent[i].wait_send()
                drained.add(i)

    drained = set()
    local = {}

    def rows_loop(first, last):
        return pl.loop(first // ROWS, last // ROWS)

    def pad():
        @rows_loop(0, BAND)
        def _(r):
            base = pl.multiple_of(r * ROWS, ROWS)
            for t in range(NT):
                npad[t, pl.ds(base + 8, ROWS), :] = noisy[pl.ds(base, ROWS), t, :].astype(F32)

    def own_cot():
        @rows_loop(0, BAND)
        def _(r):
            rows = pl.ds(pl.multiple_of(r * ROWS, ROWS), ROWS)
            for t in range(NT):
                ca[t, rows, :] = cot[rows, t, :]

    barrier = pltpu.get_barrier_semaphore()
    greeted = [f(k) for f in (me.q, me.xp, me.yp, me.zp) for k in (1, 2, 3)]
    greeted += [me.band(1), me.band(-1), me.zo(3)] + [me.zx(m) for m in (1, 2, 3)]

    def greet():
        for peer in greeted:
            pl.semaphore_signal(barrier, inc=1, device_id=peer, device_id_type=MESH)

    def enter():
        pl.semaphore_wait(barrier, len(greeted))

    def halo():
        send("halo", npad.at[:, pl.ds(8, 8), :], npad.at[:, pl.ds(BAND + 8, 8), :], me.band(-1))
        send("halo", npad.at[:, pl.ds(BAND, 8), :], npad.at[:, pl.ds(0, 8), :], me.band(1))

    def ca_slot(k, t):
        return ca.at[t, pl.ds(k * BAND, BAND), :]

    def cots():
        for t in range(NT):
            send(("cotz", t), ca_slot(0, t), ca_slot(2, t), me.q(2))
        for t in range(NT):
            send("cot", ca_slot(0, t), ca_slot(1, t), me.q(1))

    def mix_cols(k, j):
        zl, c = me.qpos(k)
        band = zl * 8 + ((me.x + j) % 4) * 2 + c
        return mixing.at[:, pl.ds(pl.multiple_of(band * BAND, BAND), BAND)]

    def mix_slot(k, j):
        return mx.at[pl.ds(k * BAND, BAND), pl.ds(j * BAND, BAND)]

    def mix():
        for j in (2, 1, 3, 0):
            for k in (1, 2, 3):
                peer = me.q(k) if k == 1 else me.zo(k)
                send(("mix", j), mix_cols(k, j), mix_slot(k, j), peer)

    def locals_in():
        for j in range(4):
            local[j] = pltpu.make_async_copy(mix_cols(0, j), mix_slot(0, j), lsem.at[j])
        for copy in local.values():
            copy.start()

    def locals_done():
        for copy in local.values():
            copy.wait()

    def halo_rows():
        arrive("halo")
        for t in range(NT):
            npad[t, 0:8, :] = npad[t, 0:8, :] * low_on
            npad[t, BAND + 8 : BAND + 16, :] = npad[t, BAND + 8 : BAND + 16, :] * high_on

    def noisy_windows(base):
        wins = []
        for t in range(NT):
            w = npad[t, pl.ds(base, ROWS + 16), :]
            wins.append([w[7 + i : 7 + i + ROWS] for i in range(3)])
        return wins

    def gate_rows(slot, first, last):
        return ga.at[:, pl.ds(slot * BAND + first, last - first), :]

    def forward(first, last):
        @rows_loop(first, last)
        def _(r):
            base = pl.multiple_of(r * ROWS, ROWS)
            wins = noisy_windows(base)
            for t in range(NT):
                st = None
                for tp in range(NT):
                    for i in range(3):
                        term = kern[i, tp - t + 1 : tp - t + 2, :] * wins[tp][i]
                        st = term if st is None else st + term
                ri = lax.rsqrt(jnp.mean(st * st, axis=-1, keepdims=True) + 1e-05)
                nm = st * ri
                normed[t, pl.ds(base, ROWS), :] = nm
                rinv[t, pl.ds(base, ROWS), :] = jnp.broadcast_to(ri, (ROWS, 128))
                act = nm * scale1 + shift
                ga[t, pl.ds(base, ROWS), :] = (act * sigmoid(act)).astype(BF16)

    def gate_send(first, last):
        h = first // half + (0 if last - first > ROWS else 2)
        send(("ga3", h), gate_rows(0, first, last), gate_rows(3, first, last), me.xp(1))
        send(("ga1", h), gate_rows(0, first, last), gate_rows(1, first, last), me.xp(3))

    def gate_right(first, last):
        arrive(("ga3", 0 if last - first > ROWS else 2))
        send("ga2", gate_rows(3, first, last), gate_rows(2, first, last), me.xp(1))

    def gate_left(first, last):
        arrive(("ga1", 1 if last - first > ROWS else 3))
        send("ga2", gate_rows(1, first, last), gate_rows(2, first, last), me.xp(3))

    def gate_all(*slots):
        for slot in slots:
            if slot == 2:
                arrive("ga2")
            else:
                arrive(*[("ga3" if slot == 3 else "ga1", h) for h in range(4)])

    def cot_pass(t):
        arrive(("cotz", t))
        send("cot", ca_slot(2, t), ca_slot(3, t), me.q(1))

    def cot_done():
        arrive("cot")
        locals_done()

    def gm_product(j):
        if j > 0:
            gate_all(j)
        acc = None
        for t in range(NT):
            part = lax.dot_general(
                ca[t], ga[t, pl.ds(j * BAND, BAND), :],
                (((1,), (1,)), ((), ())), preferred_element_type=F32,
            )
            acc = part if acc is None else acc + part
        gms[j] = acc.astype(BF16).reshape(4, BAND, BAND)

    def y_rows(m):
        return pl.ds(pl.multiple_of((me.y + m) % 4 * 64, 64), 64)

    def gm_send(j):
        near, far, back = y_rows(1), y_rows(2), y_rows(3)
        send(("ya", j), gms.at[j, pl.ds(0, 2), far, :], ymid.at[j, 0], me.yp(1))
        send(("yb", j), gms.at[j, pl.ds(2, 2), far, :], ymid.at[j, 1], me.yp(3))
        send(("y", j), gms.at[j, pl.ds(2, 2), near, :], yr.at[j, 0, pl.ds(2, 2)], me.yp(1))
        send(("y", j), gms.at[j, pl.ds(0, 2), back, :], yr.at[j, 1, pl.ds(0, 2)], me.yp(3))

    def y_join(j):
        for side, group, rows in ((0, ("ya", j), y_rows(1)), (1, ("yb", j), y_rows(3))):
            arrive(group)
            for k in range(2):
                total = gms[j, 2 * side + k, rows, :].astype(F32) + ymid[j, side, k].astype(F32)
                yout[j, side, k] = total.astype(BF16)
            send(
                ("y", j), yout.at[j, side], yr.at[j, side, pl.ds(2 * side, 2)],
                me.yp(1 if side == 0 else 3),
            )

    def y_sum(j):
        arrive(("y", j))
        for k in range(4):
            total = gms[j, k, yrows, :].astype(F32)
            for m in range(2):
                total = total + yr[j, m, k].astype(F32)
            ys[j, k] = total.astype(BF16)
        for m in (2, 1, 3, 0):
            rows = pl.ds(pl.multiple_of((me.zh + m) % 4 * 16, 16), 16)
            send(("z", j), ys.at[j, pl.ds(2, 2), rows, :], zr.at[j, 3 + m], me.zx(m))
            if m > 0:
                send(("z", j), ys.at[j, pl.ds(0, 2), rows, :], zr.at[j, m - 1], me.zp(m))

    def z_sum(j):
        arrive(("z", j))
        for far in range(2):
            for k in range(2):
                if far:
                    total = zr[j, 3, k].astype(F32)
                else:
                    total = ys[j, k, zrows, :].astype(F32)
                for m in range(3):
                    total = total + zr[j, 4 * far + m, k].astype(F32)
                if k == 0:
                    gm_o[j, mine, pl.ds(2 * far * BAND, BAND)] = total.astype(BF16)
                else:
                    zs[j, far] = total.astype(BF16)
        for far in range(2):
            cols = pl.ds((2 * far + 1) * BAND, BAND)
            send(("f", j), zs.at[j, far], gm_o.at[j, mine, cols], me.q(1))

    def z_gather(j):
        arrive(("f", j))
        for m in (2, 1, 3):
            send(("az", j), gm_o.at[j, mine], gm_o.at[j, mine], me.zp(m))

    def y_gather(j):
        arrive(("az", j))
        send(("ar", j), gm_o.at[j, yrows], gm_o.at[j, yrows], me.yp(1))
        send(("al", j), gm_o.at[j, yrows], gm_o.at[j, yrows], me.yp(3))

    def y_pass(j):
        for group, m, first, to in ((("ar", j), 3, 0, 1), (("al", j), 1, 32, 3)):
            arrive(group)
            rows = pl.ds(pl.multiple_of((me.y + m) % 4 * 64 + first, 32), 32)
            send(("ay", j), gm_o.at[j, rows], gm_o.at[j, rows], me.yp(to))

    def gate_grad(j):
        arrive(("mix", j))
        mt = mx[:, pl.ds(j * BAND, BAND)].T
        for t in range(NT):
            part = jnp.dot(mt, ca[t], preferred_element_type=F32)
            if j == 0:
                pown[t] = part
            else:
                psend[j - 1, t] = part.astype(BF16)

    def p_far():
        send("pa0", psend.at[1, 0], pmid.at[0], me.xp(1))
        send("pa1", psend.at[1, 1], pmid.at[1], me.xp(3))

    def p_right():
        send("p", psend.at[0, 1], precv.at[0, 1], me.xp(1))

    def p_left():
        send("p", psend.at[2, 0], precv.at[1, 0], me.xp(3))

    def p_join():
        arrive("pa0")
        psend[0, 0] = (psend[0, 0].astype(F32) + pmid[0].astype(F32)).astype(BF16)
        send("p", psend.at[0, 0], precv.at[0, 0], me.xp(1))
        arrive("pa1")
        psend[2, 1] = (psend[2, 1].astype(F32) + pmid[1].astype(F32)).astype(BF16)
        send("p", psend.at[2, 1], precv.at[1, 1], me.xp(3))

    def mixed(k, t):
        return jnp.dot(mx[pl.ds(k * BAND, BAND), :], ga[t], preferred_element_type=F32)

    def mixed_far():
        gate_all(1, 2, 3)
        arrive(*[("mix", j) for j in range(4)])
        for t in range(NT):
            osend[2, t] = mixed(3, t).astype(BF16)
        send("oc", osend.at[2], ocore, me.q(1))

    def mixed_core():
        for t in range(NT):
            osend[0, t] = mixed(1, t).astype(BF16)
        send("o", osend.at[0], orecv.at[0], me.q(1))

    def mixed_z():
        parts = [mixed(2, t) for t in range(NT)]
        arrive("oc")
        for t in range(NT):
            osend[1, t] = (parts[t] + ocore[t].astype(F32)).astype(BF16)
        send("o", osend.at[1], orecv.at[1], me.q(2))

    def mixed_own():
        for t in range(NT):
            oown[t] = mixed(0, t)

    def output():
        arrive("o")

        @rows_loop(0, BAND)
        def _(r):
            base = pl.multiple_of(r * ROWS, ROWS)
            rows = pl.ds(base, ROWS)
            for t in range(NT):
                total = oown[t, rows, :] + npad[t, pl.ds(base + 8, ROWS), :]
                for m in range(2):
                    total = total + orecv[m, t, rows, :].astype(F32)
                out_o[t, rows, :] = total.astype(BF16)

    def backward():
        arrive("p")
        gkacc[...] = jnp.zeros_like(gkacc)

        @rows_loop(0, BAND)
        def _(r):
            base = pl.multiple_of(r * ROWS, ROWS)
            rows = pl.ds(base, ROWS)
            wins = noisy_windows(base)
            for t in range(NT):
                gg = pown[t, rows, :]
                for m in range(2):
                    gg = gg + precv[m, t, rows, :].astype(F32)
                nm = normed[t, rows, :]
                ri = rinv[t, rows, :][:, 0:1]
                act = nm * scale1 + shift
                sig = sigmoid(act)
                gact = gg * sig * (1.0 + act * (1.0 - sig))
                prod = gact * nm
                gkacc[9] += prod[0:8] + prod[8:16]
                gkacc[10] += gact[0:8] + gact[8:16]
                gnm = gact * scale1
                mean = jnp.mean(gnm * nm, axis=-1, keepdims=True)
                gst = ri * (gnm - nm * mean)
                gs[t, pl.ds(base + 8, ROWS), :] = gst
                for tp in range(NT):
                    for i in range(3):
                        prod = wins[tp][i] * gst
                        gkacc[i * 3 + tp - t + 1] += prod[0:8] + prod[8:16]

    def grad_halo():
        send("gs", gs.at[:, pl.ds(8, 8), :], gs.at[:, pl.ds(BAND + 8, 8), :], me.band(-1))
        send("gs", gs.at[:, pl.ds(BAND, 8), :], gs.at[:, pl.ds(0, 8), :], me.band(1))

    def sums_q():
        sm[...] = jnp.zeros_like(sm)
        for i in range(11):
            sm[i : i + 1, :] = jnp.sum(gkacc[i], axis=0, keepdims=True)
        for k in (2, 3, 1):
            send("smq", sm, smq.at[k - 1], me.q(k))

    def sums_x():
        arrive("smq")
        smt[...] = sm[...] + smq[0] + smq[1] + smq[2]
        for k in (2, 1, 3):
            send("smx", smt, smx.at[k - 1], me.xp(k))

    def sums_y():
        arrive("smx")
        smr[...] = smt[...] + smx[0] + smx[1] + smx[2]
        smy[me.y] = smr[...]
        for m in (2, 1, 3):
            send("gy", smr, smy.at[me.y], me.yp(m))

    def sums_z():
        arrive("gy")
        smz[...] = jnp.zeros_like(smz)
        smz[0:16] = smy[0] + smy[1] + smy[2] + smy[3]
        for y in range(4):
            for i in range(2):
                smz[16 + 4 * i + y : 17 + 4 * i + y, :] = smy[y, 9 + i : 10 + i, :]
        gat_o[me.zh] = smz[...]
        for m in (2, 1, 3):
            send("gz", smz, gat_o.at[me.zh], me.zp(m))

    def embeds_y():
        eg_o[me.dp] = embed[...]
        for m in (2, 1, 3):
            send("ey", embed, eg_o.at[me.dp], me.yp(m))

    def embeds_z():
        arrive("ey")
        for m in (2, 1, 3):
            send("ez", eg_o.at[four], eg_o.at[four], me.zp(m))

    def grad_back():
        arrive("gs")
        for t in range(NT):
            gs[t, 0:8, :] = gs[t, 0:8, :] * low_on
            gs[t, BAND + 8 : BAND + 16, :] = gs[t, BAND + 8 : BAND + 16, :] * high_on

        @rows_loop(0, BAND)
        def _(r):
            base = pl.multiple_of(r * ROWS, ROWS)
            rows = pl.ds(base, ROWS)
            wins = []
            for t in range(NT):
                w = gs[t, pl.ds(base, ROWS + 16), :]
                wins.append([w[9 - i : 9 - i + ROWS] for i in range(3)])
            for tp in range(NT):
                back = ca[tp, rows, :].astype(F32)
                for t in range(NT):
                    for i in range(3):
                        back = back + kern[i, tp - t + 1 : tp - t + 2, :] * wins[t][i]
                gn_o[tp, rows, :] = back.astype(BF16)

    def gm_done(j):
        arrive(("ay", j))
        local_out.append(pltpu.make_async_copy(gm_o.at[j], gm_h.at[j], osem.at[j]))
        local_out[-1].start()

    def out_done():
        local_out.append(pltpu.make_async_copy(out_o, out_h, osem.at[4]))
        local_out[-1].start()

    def back_done():
        local_out.append(pltpu.make_async_copy(gn_o, gn_h, osem.at[5]))
        local_out[-1].start()

    local_out = []
    order(types.SimpleNamespace(**locals()))
    for name in list(groups):
        arrive(name)
    all_sent()
    for copy in local_out:
        copy.wait()


N_COPIES = 2 + 6 + 12 + 12 + 6 + 3 + 4 * (6 + 7 + 2 + 3 + 4) + 2 + 12 + 6


def schedule(k):
    k.greet()
    k.pad()
    k.own_cot()
    k.forward(16, 240)
    k.enter()
    k.halo()
    k.gate_send(16, 128)
    k.gate_send(128, 240)
    k.cots()
    k.halo_rows()
    k.forward(0, 16)
    k.forward(240, 256)
    k.gate_send(0, 16)
    k.gate_send(240, 256)
    k.mix()
    k.locals_in()
    k.embeds_y()
    k.gate_right(16, 128)
    k.cot_pass(0)
    k.embeds_z()
    k.gate_left(128, 240)
    k.cot_pass(1)
    k.gate_right(0, 16)
    k.gate_left(240, 256)
    k.cot_done()
    k.gm_product(0)
    k.gm_send(0)
    k.gm_product(3)
    k.gm_send(3)
    k.gm_product(1)
    k.gm_send(1)
    k.gate_grad(2)
    k.p_far()
    k.y_join(0)
    k.y_join(3)
    k.y_sum(0)
    k.gm_product(2)
    k.gm_send(2)
    k.gate_grad(1)
    k.p_right()
    k.gate_grad(3)
    k.p_left()
    k.y_join(1)
    k.p_join()
    k.gate_grad(0)
    k.z_sum(0)
    k.y_sum(3)
    k.y_join(2)
    k.mixed_far()
    k.y_sum(1)
    k.z_gather(0)
    k.z_sum(3)
    k.mixed_core()
    k.y_sum(2)
    k.mixed_own()
    k.y_gather(0)
    k.z_gather(3)
    k.z_sum(1)
    k.y_gather(3)
    k.z_gather(1)
    k.z_sum(2)
    k.y_pass(0)
    k.backward()
    k.grad_halo()
    k.sums_q()
    k.z_gather(2)
    k.y_gather(1)
    k.y_pass(3)
    k.mixed_z()
    k.sums_x()
    k.y_gather(2)
    k.y_pass(1)
    k.grad_back()
    k.back_done()
    k.sums_y()
    k.y_pass(2)
    k.sums_z()
    k.output()
    k.out_done()
    k.gm_done(0)
    k.gm_done(3)
    k.gm_done(1)
    k.gm_done(2)


def fused_block(noisy, cot, mixing, film, embed, kern, order=schedule, number=0):
    vmem = pl.BlockSpec(memory_space=pltpu.VMEM)
    hbm = pl.BlockSpec(memory_space=pl.ANY)
    act = (NT, BAND, C)
    full = (NT, 4 * BAND, C)
    pad = (NT, BAND + 16, C)
    return pl.pallas_call(
        functools.partial(block_kernel, order=order),
        out_shape=(
            jax.ShapeDtypeStruct(act, BF16),
            jax.ShapeDtypeStruct(act, BF16),
            jax.ShapeDtypeStruct((4, BAND, 4 * BAND), BF16),
            jax.ShapeDtypeStruct((4, 24, C), F32),
            jax.ShapeDtypeStruct((16, 1, C), F32),
        ),
        in_specs=[vmem, vmem, hbm, vmem, vmem, vmem],
        out_specs=(hbm,) * 3 + (vmem,) * 2,
        scratch_shapes=[
            pltpu.VMEM(act, BF16),
            pltpu.VMEM(act, BF16),
            pltpu.VMEM((4, BAND, 4 * BAND), BF16),
            pltpu.VMEM(pad, F32),
            pltpu.VMEM(act, F32),
            pltpu.VMEM((NT, BAND, 128), F32),
            pltpu.VMEM(full, BF16),
            pltpu.VMEM(full, BF16),
            pltpu.VMEM((4 * BAND, 4 * BAND), BF16),
            pltpu.VMEM((3,) + act, BF16),
            pltpu.VMEM(act, BF16),
            pltpu.VMEM((2,) + act, BF16),
            pltpu.VMEM(act, F32),
            pltpu.VMEM((3,) + act, BF16),
            pltpu.VMEM((2,) + act, BF16),
            pltpu.VMEM(act, BF16),
            pltpu.VMEM(act, F32),
            pltpu.VMEM((4, 4, BAND, BAND), BF16),
            pltpu.VMEM((4, 2, 2, 64, BAND), BF16),
            pltpu.VMEM((4, 2, 2, 64, BAND), BF16),
            pltpu.VMEM((4, 2, 4, 64, BAND), BF16),
            pltpu.VMEM((4, 4, 64, BAND), BF16),
            pltpu.VMEM((4, 7, 2, 16, BAND), BF16),
            pltpu.VMEM((4, 2, 16, BAND), BF16),
            pltpu.VMEM(pad, F32),
            pltpu.VMEM((11, 8, C), F32),
            pltpu.VMEM((16, C), F32),
            pltpu.VMEM((3, 16, C), F32),
            pltpu.VMEM((3, 16, C), F32),
            pltpu.VMEM((16, C), F32),
            pltpu.VMEM((16, C), F32),
            pltpu.VMEM((4, 16, C), F32),
            pltpu.VMEM((24, C), F32),
            pltpu.SemaphoreType.DMA((N_COPIES,)),
            pltpu.SemaphoreType.DMA((N_COPIES,)),
            pltpu.SemaphoreType.DMA((4,)),
            pltpu.SemaphoreType.DMA((6,)),
        ],
        compiler_params=pltpu.CompilerParams(
            collective_id=number, has_side_effects=True, vmem_limit_bytes=60 * 1024 * 1024
        ),
    )(noisy, cot, mixing, film, embed, kern)


def finish_kernel(out, gn, gm, gat, eg, out_o, gn_o, gm_o, gk_o, film_o):
    step = pl.program_id(0)
    fr = lax.axis_index("freq")
    zl, x, c = fr // 8, (fr // 2) % 4, fr % 2
    for src, dst in ((out, out_o), (gn, gn_o)):
        rows = src.shape[1]
        row = lax.broadcasted_iota(jnp.int32, (2 * rows, rows), 0)
        col = lax.broadcasted_iota(jnp.int32, (2 * rows, rows), 1)
        pairs = None
        for t in range(NT):
            pick = (row == 2 * col + t).astype(F32).astype(BF16)
            part = jnp.dot(pick, src[t], preferred_element_type=F32)
            pairs = part if pairs is None else pairs + part
        dst[...] = pairs.astype(BF16).reshape(rows, NT, C)
    for k in range(4):
        bz = zl if k < 2 else 1 - zl
        bc = c if k % 2 == 0 else 1 - c
        for j in range(4):
            band = bz * 8 + ((x + j) % 4) * 2 + bc
            cols = pl.ds(pl.multiple_of(band * BAND, BAND), BAND)
            gm_o[:, cols] = gm[j, :, k * BAND : (k + 1) * BAND].astype(F32)
    wide = film_o.shape[0]
    embeds = eg[:, 0, pl.ds(pl.multiple_of(step * wide, wide), wide)]
    both = jnp.concatenate(
        [jnp.concatenate([gat[z, 16 + 4 * i : 20 + 4 * i] for z in range(4)]) for i in range(2)],
        axis=1,
    )
    parts = []
    for _ in range(3):
        parts.append(both.astype(BF16))
        both = both - parts[-1].astype(F32)
    film_o[...] = lax.dot_general(
        jnp.concatenate([embeds.astype(BF16)] * 3), jnp.concatenate(parts),
        (((0,), (0,)), ((), ())), preferred_element_type=F32,
    )

    @pl.when(step == 0)
    def _():
        total = jnp.sum(gat[:, 0:9, :], axis=0)
        for i in range(3):
            gk_o[i] = total[3 * i : 3 * i + 3]


def finish(out, grad_noisy, grad_mixing, sums, embeds):
    steps = 4
    rows, wide = BAND // steps, C // steps
    planes = pl.BlockSpec((NT, rows, C), lambda i: (0, i, 0))
    pairs = pl.BlockSpec((rows, NT, C), lambda i: (i, 0, 0))
    return pl.pallas_call(
        finish_kernel,
        grid=(steps,),
        out_shape=(
            jax.ShapeDtypeStruct((BAND, NT, C), BF16),
            jax.ShapeDtypeStruct((BAND, NT, C), BF16),
            jax.ShapeDtypeStruct((BAND, 16 * BAND), F32),
            jax.ShapeDtypeStruct((3, 3, C), F32),
            jax.ShapeDtypeStruct((C, 2 * C), F32),
        ),
        in_specs=[
            planes,
            planes,
            pl.BlockSpec((4, rows, 4 * BAND), lambda i: (0, i, 0)),
            pl.BlockSpec((4, 24, C), lambda i: (0, 0, 0)),
            pl.BlockSpec((16, 1, C), lambda i: (0, 0, 0)),
        ],
        out_specs=(
            pairs,
            pairs,
            pl.BlockSpec((rows, 16 * BAND), lambda i: (i, 0)),
            pl.BlockSpec((3, 3, C), lambda i: (0, 0, 0)),
            pl.BlockSpec((wide, 2 * C), lambda i: (i, 0)),
        ),
        compiler_params=pltpu.CompilerParams(vmem_limit_bytes=60 * 1024 * 1024),
    )(out, grad_noisy, grad_mixing, sums, embeds)


def embed_steps(timestep, width):
    half = width // 2
    freqs = jnp.exp(-math.log(10000.0) * jnp.arange(half, dtype=jnp.float32) / half)
    angles = timestep.astype(jnp.float32)[:, None] * freqs[None, :]
    return jnp.concatenate([jnp.sin(angles), jnp.cos(angles)], axis=1).astype(jnp.bfloat16)


def on_device(noisy, timestep, kernel, film_weight, mixing, cotangent):
    embed = embed_steps(timestep, C)
    film = jnp.dot(embed, film_weight, preferred_element_type=jnp.float32)
    film = jnp.concatenate([1.0 + film[:, :C], film[:, C:]], axis=0)
    out, grad_noisy, grad_mixing, sums, embeds = fused_block(
        noisy[0], cotangent[0], mixing, film, embed.astype(F32), kernel
    )
    output, grad_noisy, grad_mixing, grad_kernel, grad_film = finish(
        out, grad_noisy, grad_mixing, sums, embeds
    )
    output, grad_noisy = output[None], grad_noisy[None]
    return (output, grad_noisy, grad_mixing, grad_kernel, grad_film)


def solution(mesh):
    return jax.shard_map(
        on_device,
        mesh=mesh,
        in_specs=(
            P("dp", "freq", None, None),
            P("dp"),
            P(),
            P(),
            P("freq", None),
            P("dp", "freq", None, None),
        ),
        out_specs=(
            P("dp", "freq", None, None),
            P("dp", "freq", None, None),
            P("freq", None),
            P(),
            P(),
        ),
        check_vma=False,
    )
```
